128 devices in a mesh: tx: 8 (over z_hi, y), ty: 16 (over x, z_lo, core).
Axes of the slice: x: 4, y: 4, z: 4 (z_hi: 2, z_lo: 2; z = z_hi * 2 + z_lo), core: 2. Of those that a mesh axis runs over, the one named last changes fastest.
Arguments:
- states: bfloat16 [2, 256, 16384], P(None, 'ty', 'tx')
- norm_gain: bfloat16 [16384], P('tx'), may hold values from 0.099609375 to 1.8984375
- w_gate: bfloat16 [16384, 26624], P('tx', 'ty'), may hold values from -0.046875 to 0.046875
- w_up: bfloat16 [16384, 26624], P('tx', 'ty'), may hold values from -0.046875 to 0.046875
- w_down: bfloat16 [26624, 16384], P('ty', 'tx'), may hold values from -0.0390625 to 0.0390625
- w_qkv: bfloat16 [16384, 3, 4096], P('tx', None, 'ty'), may hold values from -0.046875 to 0.046875
- w_class: bfloat16 [4096, 14], P('ty'), may hold values from -0.375 to 0.375
- cache_keys: bfloat16 [256, 64, 4096], P('tx', None, 'ty')
- cache_values: bfloat16 [256, 64, 4096], P('tx', None, 'ty'), may hold values from -6 to 6
- cache_lengths: int32 [256], P('tx'), may hold values from 1 to 64, as said below
- row_slots: int32 [256], replicated, may hold values from 0 to 255, each once
Outputs:
- stream_out: bfloat16 [2, 256, 16384], P(None, 'ty', 'tx')
- category_logits: float32 [2, 256, 14], replicated
The draws below stay inside these ranges and needn't reach their ends.
Inputs may be any that keep to these rules, and one draw needn't show every extreme that they name: `cache_lengths`: some slot has exactly 64 live positions. `row_slots`: each cache slot belongs to exactly one row.
All inputs are finite; a program needn't handle non-finite values.
Results may differ from the reference program's by a relative error of at most 0.015.
The reference program's roundings to bfloat16 on the way count: a program that leaves them out, or rounds other values in their place, can miss the bound.
Values may be sent and summed in bfloat16 or wider, within the bound.
No kernel may reach another device: no remote copies, remote signals or barrier semaphores. Data moves between devices by JAX's collectives and lax.ppermute only.
A program may use at most 128 MiB of HBM per device.

```python
import jax
import jax.numpy as jnp
from jax import lax

D = 16384
FF = 26624
CW = 4096
HEAD_DIM = 128
CLASSES = 14
STEPS = 2
CACHE = 64
ROWS = 256


def draw_states(key, part):
    first, second, third = jax.random.split(jax.random.fold_in(key, 11), 3)
    columns = jnp.arange(D, dtype=jnp.float32) / D
    col_scale = jnp.exp(jnp.log(3.0) * columns) * jax.random.uniform(second, (D,), jnp.float32, 0.6, 1.4)
    row_scale = jnp.exp(jax.random.uniform(third, (STEPS, ROWS, 1), jnp.float32, jnp.log(0.3), jnp.log(3.0)))
    base = jax.random.normal(first, (STEPS, ROWS, D), jnp.float32)
    base = jnp.clip(base, -6.0, 6.0)
    return (base * col_scale * row_scale).astype(jnp.bfloat16)


def draw_cache_keys(key, part):
    first = jax.random.fold_in(jax.random.fold_in(key, 23), 0)
    base = jnp.clip(jax.random.normal(first, (ROWS, CACHE, CW), jnp.float32), -6.0, 6.0)
    return base.astype(jnp.bfloat16)


def draw_cache_lengths(key, part):
    first, second = jax.random.split(jax.random.fold_in(key, 37), 2)
    lengths = jax.random.randint(first, (ROWS,), 1, CACHE + 1)
    spot = jax.random.randint(second, (), 0, ROWS)
    return jnp.where(jnp.arange(ROWS) == spot, CACHE, lengths).astype(jnp.int32)


def levels(own_key, shape, pieces, smallest, top_value):
    level = 1.0
    for position, parts in pieces:
        draws = jax.random.uniform(jax.random.fold_in(jax.random.fold_in(own_key, 6), position), (parts,), jnp.float32, smallest / len(pieces), top_value / len(pieces))
        level = level * jnp.repeat(jnp.exp(draws), shape[position] // parts).reshape((-1,) + (1,) * (len(shape) - 1 - position))
    return level


def centred(rng, shape, deviation, limit, shards=(), held_as=jnp.bfloat16):
    level = levels(rng, shape, shards, -0.22, 0.18) if shards else 1.0
    array = jax.random.normal(rng, shape, jnp.float32) * deviation * level
    return jnp.minimum(jnp.maximum(array, -limit), limit).astype(held_as)


def setup_inputs(seed: int = 0) -> dict:
    streams_of = jax.random.split(jax.random.key(seed), 12)
    return {
        "states": draw_states(jax.random.fold_in(streams_of[11], 71), 0),
        "norm_gain": jnp.clip(1.0 + 0.18 * jax.random.normal(streams_of[1], (D,), jnp.float32), 0.099609375, 1.8984375).astype(jnp.bfloat16),
        "w_gate": centred(streams_of[2], (D, FF), D ** -0.5, 0.046875, ((0, 8), (1, 16))),
        "w_up": centred(streams_of[3], (D, FF), D ** -0.5, 0.046875, ((0, 8), (1, 16))),
        "w_down": centred(streams_of[4], (FF, D), FF ** -0.5, 0.0390625, ((0, 16), (1, 8))),
        "w_qkv": centred(streams_of[5], (D, 3, CW), D ** -0.5, 0.046875, ((0, 8), (2, 16))),
        "w_class": centred(streams_of[6], (CW, CLASSES), (CW // 16) ** -0.5, 0.375, ((0, 16),)),
        "cache_keys": draw_cache_keys(jax.random.fold_in(streams_of[11], 71), 0),
        "cache_values": centred(streams_of[8], (ROWS, CACHE, CW), 1.0, 6.0, ((0, 8), (2, 16))),
        "cache_lengths": draw_cache_lengths(jax.random.fold_in(streams_of[11], 71), 0),
        "row_slots": jax.random.permutation(streams_of[10], ROWS).astype(jnp.int32),
    }


def reference(states, norm_gain, w_gate, w_up, w_down, w_qkv, w_class, cache_keys, cache_values, cache_lengths, row_slots):
    total_rows = states.shape[1]
    slot_rows = jnp.zeros((total_rows,), jnp.int32).at[row_slots].set(jnp.arange(total_rows, dtype=jnp.int32))
    history = cache_keys.shape[1]
    heads = CW // HEAD_DIM
    qkv_weight = w_qkv.reshape(D, 3 * CW)
    gain = norm_gain.astype(jnp.float32)
    outputs = []
    logits_all = []
    new_keys = []
    new_values = []
    for step in range(STEPS):
        values_f = states[step].astype(jnp.float32)
        scale = lax.rsqrt(lax.optimization_barrier(jnp.mean(values_f * values_f, axis=1, keepdims=True)) + 1e-05)
        normed = (values_f * scale * gain).astype(jnp.bfloat16)
        gate = jnp.dot(normed, w_gate, preferred_element_type=jnp.float32)
        up = jnp.dot(normed, w_up, preferred_element_type=jnp.float32)
        hidden = (jax.nn.silu(gate) * up).astype(jnp.bfloat16)
        stream = (values_f + jnp.dot(hidden, w_down, preferred_element_type=jnp.float32)).astype(jnp.bfloat16)
        outputs.append(stream)
        ordered = jnp.take(stream, slot_rows, axis=0)
        triple = jnp.dot(ordered, qkv_weight, preferred_element_type=jnp.float32).astype(jnp.bfloat16).reshape(total_rows, 3, CW)
        query = triple[:, 0]
        new_keys.append(triple[:, 1])
        new_values.append(triple[:, 2])
        keys = jnp.concatenate([cache_keys, jnp.stack(new_keys, axis=1)], axis=1)
        vals = jnp.concatenate([cache_values, jnp.stack(new_values, axis=1)], axis=1)
        count_keys = keys.shape[1]
        query_h = query.astype(jnp.float32).reshape(total_rows, heads, HEAD_DIM)
        keys_h = keys.astype(jnp.float32).reshape(total_rows, count_keys, heads, HEAD_DIM)
        vals_h = vals.astype(jnp.float32).reshape(total_rows, count_keys, heads, HEAD_DIM)
        scores = jnp.einsum('shd,slhd->shl', query_h, keys_h) * HEAD_DIM ** (-0.5)
        where_pos = jnp.arange(count_keys, dtype=jnp.int32)
        valid = (where_pos[None, :] < cache_lengths[:, None]) | (where_pos[None, :] >= history)
        scores = jnp.where(valid[:, None, :], scores, jnp.float32(-1e+30))
        top = lax.optimization_barrier(jnp.max(scores, axis=2, keepdims=True))
        expo = jnp.exp(scores - top)
        weights = (expo / lax.optimization_barrier(jnp.sum(expo, axis=2, keepdims=True))).astype(jnp.bfloat16)
        attended = jnp.einsum('shl,slhd->shd', weights.astype(jnp.float32), vals_h)
        attended = attended.reshape(total_rows, CW).astype(jnp.bfloat16)
        by_slot = jnp.dot(attended, w_class, preferred_element_type=jnp.float32)
        logits_all.append(jnp.take(by_slot, row_slots, axis=0))
    return (jnp.stack(outputs, axis=0), jnp.stack(logits_all, axis=0))
```

```python
import functools

import jax
import jax.numpy as jnp
from jax import lax
from jax.experimental import pallas as pl
from jax.experimental.pallas import tpu as pltpu
from jax.sharding import PartitionSpec as P

D = 16384
HEAD_DIM = 128
DOWN = 2.0 ** -24
UP = 2.0 ** 24
MOVES = [(d, dz) for dz in range(2) for d in range(4)]
LIMIT = 24 * 1024 * 1024


def tx_move(array, dy, dz):
    pairs = [(z * 4 + y, (z ^ dz) * 4 + (y + dy) % 4) for z in range(2) for y in range(4)]
    return lax.ppermute(array, "tx", pairs)


def ty_move(array, dx, dz, dc):
    pairs = [
        (x * 4 + z * 2 + c, ((x + dx) % 4) * 4 + (z ^ dz) * 2 + (c ^ dc))
        for x in range(4)
        for z in range(2)
        for c in range(2)
    ]
    return lax.ppermute(array, "ty", pairs)


def gather_ty(rows):
    pieces = [rows] + [ty_move(rows, dx, dz, 0) for dx, dz in MOVES[1:]]
    mine = jnp.concatenate(pieces, axis=0)
    return mine, ty_move(mine, 0, 0, 1)


def f32(array):
    return array.astype(jnp.float32)


def total(blocks):
    out = f32(blocks[0])
    for block in blocks[1:]:
        out = out + f32(block)
    return out


def gate_up_kernel(order, x_ref, gain_ref, wg_ref, wu_ref, *refs):
    outs, scaled = refs[:-1], refs[-1]
    step = pl.program_id(0)
    hidden = 128 * pl.num_programs(0)
    rows = outs[0].shape[0]
    unit = x_ref.shape[0] // 8

    @pl.when(step == 0)
    def _():
        gain = gain_ref[...].astype(jnp.float32) * DOWN
        lane = lax.broadcasted_iota(jnp.int32, (unit, 128), 1)
        for n in range(8):
            start = pl.multiple_of(order[n] * unit, unit)
            values = x_ref[pl.ds(start, unit), :].astype(jnp.float32)
            scaled[n * unit : (n + 1) * unit, :] = (values * gain).astype(jnp.bfloat16)
            squares = jnp.sum(values * values, axis=1, keepdims=True)
            first = squares.astype(jnp.bfloat16).astype(jnp.float32)
            second = (squares - first).astype(jnp.bfloat16).astype(jnp.float32)
            third = squares - first - second
            columns = jnp.where(lane == 0, first, jnp.where(lane == 1, second, jnp.where(lane == 2, third, 0.0)))
            at = (n * unit) % rows
            outs[n * unit // rows][at : at + unit, 2 * hidden :] = columns.astype(jnp.bfloat16)

    weights = jnp.concatenate([wg_ref[...], wu_ref[...]], axis=1)
    result = jnp.dot(scaled[...], weights, preferred_element_type=jnp.float32).astype(jnp.bfloat16)
    at_gate = pl.multiple_of(step * 128, 128)
    at_up = pl.multiple_of(hidden + step * 128, 128)
    for n, out in enumerate(outs):
        out[:, pl.ds(at_gate, 128)] = result[n * rows : (n + 1) * rows, :128]
        out[:, pl.ds(at_up, 128)] = result[n * rows : (n + 1) * rows, 128:]


def gate_up(order, x, gain, w_gate, w_up, blocks):
    rows, width = x.shape
    hidden = w_gate.shape[1]
    out = jax.ShapeDtypeStruct((rows // blocks, 2 * hidden + 128), jnp.bfloat16)
    return pl.pallas_call(
        gate_up_kernel,
        out_shape=[out] * blocks,
        grid_spec=pltpu.PrefetchScalarGridSpec(
            num_scalar_prefetch=1,
            grid=(hidden // 128,),
            in_specs=[
                pl.BlockSpec((rows, width), lambda n, o: (0, 0)),
                pl.BlockSpec((1, width), lambda n, o: (0, 0)),
                pl.BlockSpec((width, 128), lambda n, o: (0, n)),
                pl.BlockSpec((width, 128), lambda n, o: (0, n)),
            ],
            out_specs=[pl.BlockSpec(out.shape, lambda n, o: (0, 0))] * blocks,
            scratch_shapes=[pltpu.VMEM((rows, width), jnp.bfloat16)],
        ),
        compiler_params=pltpu.CompilerParams(
            dimension_semantics=("arbitrary",), vmem_limit_bytes=LIMIT
        ),
        cost_estimate=pl.CostEstimate(
            flops=4 * rows * width * hidden, transcendentals=0, bytes_accessed=4 * width * hidden + 4 * rows * hidden
        ),
    )(order, x, gain, w_gate, w_up)


def down_kernel(order, *refs):
    pieces, w_ref, out_ref, hidden = refs[:-3], refs[-3], refs[-2], refs[-1]
    unit = hidden.shape[0] // 8

    @pl.when(pl.program_id(0) == 0)
    def _():
        per = pieces[0].shape[0] // unit
        for n in range(8):
            start = pl.multiple_of(order[n] * unit, unit)
            at = (n % per) * unit
            hidden[pl.ds(start, unit), :] = pieces[n // per][at : at + unit, :]

    out_ref[...] = jnp.dot(hidden[...], w_ref[...], preferred_element_type=jnp.float32).astype(jnp.bfloat16)


def down(order, pieces, w_down):
    rows = sum(piece.shape[0] for piece in pieces)
    inner, width = w_down.shape
    tile = 256
    return pl.pallas_call(
        down_kernel,
        out_shape=jax.ShapeDtypeStruct((rows, width), jnp.bfloat16),
        grid_spec=pltpu.PrefetchScalarGridSpec(
            num_scalar_prefetch=1,
            grid=(width // tile,),
            in_specs=[pl.BlockSpec(piece.shape, lambda n, o: (0, 0)) for piece in pieces]
            + [pl.BlockSpec((inner, tile), lambda n, o: (0, n))],
            out_specs=pl.BlockSpec((rows, tile), lambda n, o: (0, n)),
            scratch_shapes=[pltpu.VMEM((rows, inner), jnp.bfloat16)],
        ),
        compiler_params=pltpu.CompilerParams(
            dimension_semantics=("arbitrary",), vmem_limit_bytes=LIMIT
        ),
        cost_estimate=pl.CostEstimate(
            flops=2 * rows * inner * width, transcendentals=0, bytes_accessed=2 * width * (inner + rows)
        ),
    )(order, *pieces, w_down)


def qkv_kernel(mine_ref, other_ref, src_ref, dst_ref, w_ref, *refs):
    outs, ordered = refs[:-1], refs[-1]
    half = mine_ref.shape[0]
    part = pl.program_id(0)

    @pl.when(part == 0)
    def _():
        pick = jnp.where(dst_ref[...] == src_ref[...], 1.0, 0.0).astype(jnp.bfloat16)
        rows = jnp.dot(pick[:, :half], mine_ref[...], preferred_element_type=jnp.float32)
        rows = rows + jnp.dot(pick[:, half:], other_ref[...], preferred_element_type=jnp.float32)
        ordered[...] = rows.astype(jnp.bfloat16)

    result = jnp.dot(ordered[...], w_ref[0], preferred_element_type=jnp.float32).astype(jnp.bfloat16)
    block, wide = outs[0].shape[0], w_ref.shape[2]
    at = pl.multiple_of(part * wide, wide)
    for n, out in enumerate(outs):
        out[:, pl.ds(at, wide)] = result[n * block : (n + 1) * block, :]


def slot_qkv(mine, other, key_src, key_dst, w_parts, blocks):
    half, width = mine.shape
    rows = 2 * half
    parts, _, wide = w_parts.shape
    out = jax.ShapeDtypeStruct((rows // blocks, parts * wide), jnp.bfloat16)
    return pl.pallas_call(
        qkv_kernel,
        out_shape=[out] * blocks,
        grid_spec=pltpu.PrefetchScalarGridSpec(
            num_scalar_prefetch=0,
            grid=(parts,),
            in_specs=[
                pl.BlockSpec((half, width), lambda n: (0, 0)),
                pl.BlockSpec((half, width), lambda n: (0, 0)),
                pl.BlockSpec((1, rows), lambda n: (0, 0)),
                pl.BlockSpec((rows, 1), lambda n: (0, 0)),
                pl.BlockSpec((1, width, wide), lambda n: (n, 0, 0)),
            ],
            out_specs=[pl.BlockSpec(out.shape, lambda n: (0, 0))] * blocks,
            scratch_shapes=[pltpu.VMEM((rows, width), jnp.bfloat16)],
        ),
        compiler_params=pltpu.CompilerParams(
            dimension_semantics=("arbitrary",), vmem_limit_bytes=LIMIT
        ),
        cost_estimate=pl.CostEstimate(
            flops=2 * rows * width * (parts * wide + rows),
            transcendentals=0,
            bytes_accessed=2 * width * (parts * wide + rows),
        ),
    )(mine, other, key_src, key_dst, w_parts)


def per_device(
    states,
    norm_gain,
    w_gate,
    w_up,
    w_down,
    w_qkv,
    w_class,
    cache_keys,
    cache_values,
    cache_lengths,
    row_slots,
):
    steps = states.shape[0]
    local_rows = states.shape[1]
    width = states.shape[2]
    hidden_here = w_gate.shape[1]
    owner_rows = cache_keys.shape[0]
    history = cache_keys.shape[1]
    local_width = w_qkv.shape[2]
    heads_here = local_width // HEAD_DIM
    total_rows = row_slots.shape[0]
    rows = steps * total_rows
    per = steps * local_rows
    block = rows // 8
    unit = block // 2
    tx = lax.axis_index("tx")
    ty = lax.axis_index("ty")
    my_y, my_zh = tx % 4, tx // 4
    my_x, my_zl, my_c = ty // 4, (ty // 2) % 2, ty % 2

    def to(dy, dz):
        return (my_zh ^ dz) * 4 + (my_y + dy) % 4

    def source(dy, dz):
        return (my_zh ^ dz) * 4 + (my_y - dy + 4) % 4

    y_major = [(dy, dz) for dy in range(4) for dz in range(2)]
    z_major = [(dy, dz) for dz in range(2) for dy in range(4)]
    send_a = jnp.stack([to(*m) for m in y_major])
    send_b = jnp.stack([to(*m) for m in z_major])
    from_a = jnp.stack([source(*m) for m in y_major])
    from_b = jnp.stack([source(*m) for m in z_major])

    pos = jnp.arange(rows, dtype=jnp.int32)
    chunk = pos // per
    dc, dzl, dx = chunk // 8, (chunk // 4) % 2, chunk % 4
    source_ty = ((my_x - dx + 4) % 4) * 4 + (my_zl ^ dzl) * 2 + (my_c ^ dc)
    row_of = source_ty * local_rows + pos % local_rows
    hit = row_of[:, None] == jnp.arange(total_rows, dtype=jnp.int32)[None, :]
    slot_of = jnp.sum(jnp.where(hit, row_slots[None, :], 0), axis=1)
    key_src = (((pos % per) // local_rows) * total_rows + slot_of)[None, :]
    target = jnp.zeros((rows,), jnp.int32)
    for n, move in enumerate(MOVES):
        target = jnp.where(pos // block == n, to(*move), target)
    key_dst = (((pos % block) // owner_rows) * total_rows + target * owner_rows + pos % owner_rows)[:, None]

    own = states.reshape(per, width)
    gain = norm_gain[None, :]
    mine, other = gather_ty(own)
    part_a = gate_up(send_a, mine, gain, w_gate, w_up, 4)
    part_b = gate_up(send_b, other, gain, w_gate, w_up, 2)
    sum_a = total([part_a[0]] + [tx_move(part_a[dy], dy, 0) for dy in range(1, 4)])
    sum_b = total([part_b[0], tx_move(part_b[1], 0, 1)])
    sum_a = sum_a[:unit] + f32(tx_move(sum_a[unit:].astype(jnp.bfloat16), 0, 1))
    sum_b = sum_b[:unit] + total(
        [tx_move(sum_b[dy * unit : (dy + 1) * unit].astype(jnp.bfloat16), dy, 0) for dy in range(1, 4)]
    )

    def activate(summed):
        sq = summed[:, 2 * hidden_here :]
        scale = lax.rsqrt((sq[:, 0:1] + sq[:, 1:2] + sq[:, 2:3]) / D + 1e-05) * UP
        gate = summed[:, :hidden_here] * scale
        up = summed[:, hidden_here : 2 * hidden_here] * scale
        return (jax.nn.silu(gate) * up).astype(jnp.bfloat16)

    hidden_a = activate(sum_a)
    hidden_b = activate(sum_b)
    pair_a = jnp.concatenate([hidden_a, tx_move(hidden_a, 0, 1)], axis=0)
    line_b = jnp.concatenate([hidden_b] + [tx_move(hidden_b, dy, 0) for dy in range(1, 4)], axis=0)
    pieces_a = [pair_a] + [tx_move(pair_a, dy, 0) for dy in range(1, 4)]
    pieces_b = [line_b, tx_move(line_b, 0, 1)]
    mixed_b = down(from_b, pieces_b, w_down)
    mixed_a = down(from_a, pieces_a, w_down)
    pair = ty_move(mixed_b, 0, 0, 1)
    chip = (f32(mixed_a) + f32(pair)).astype(jnp.bfloat16)
    parts = []
    for n, (dx, dz) in enumerate(MOVES):
        piece = chip[n * per : (n + 1) * per]
        parts.append(piece if n == 0 else ty_move(piece, (4 - dx) % 4, dz, 0))
    stream = (f32(own) + total(parts)).astype(jnp.bfloat16)
    stream_out = stream.reshape(steps, local_rows, width)

    mine, other = gather_ty(stream)
    qkv = slot_qkv(mine, other, key_src, key_dst, jnp.transpose(w_qkv, (1, 0, 2)), 8)
    received = [piece if n == 0 else tx_move(piece, *MOVES[n]) for n, piece in enumerate(qkv)]
    triple = total(received).astype(jnp.bfloat16).reshape(steps, owner_rows, 3, heads_here, HEAD_DIM)
    query, new_keys, new_vals = triple[:, :, 0], triple[:, :, 1], triple[:, :, 2]
    keys_h = cache_keys.reshape(owner_rows, history, heads_here, HEAD_DIM)
    vals_h = cache_values.reshape(owner_rows, history, heads_here, HEAD_DIM)
    old = jnp.einsum("tshd,slhd->tshl", query, keys_h, preferred_element_type=jnp.float32)
    new = jnp.einsum("tshd,ushd->tshu", query, new_keys, preferred_element_type=jnp.float32)
    old = old * HEAD_DIM ** (-0.5)
    new = new * HEAD_DIM ** (-0.5)
    where_pos = jnp.arange(history, dtype=jnp.int32)
    old = jnp.where((where_pos[None, :] < cache_lengths[:, None])[None, :, None, :], old, jnp.float32(-1e30))
    causal = jnp.arange(steps)[:, None] >= jnp.arange(steps)[None, :]
    new = jnp.where(causal[:, None, None, :], new, jnp.float32(-1e30))
    top = jnp.maximum(jnp.max(old, axis=3, keepdims=True), jnp.max(new, axis=3, keepdims=True))
    old = jnp.exp(old - top)
    new = jnp.exp(new - top)
    denom = jnp.sum(old, axis=3, keepdims=True) + jnp.sum(new, axis=3, keepdims=True)
    old = (old / denom).astype(jnp.bfloat16)
    new = (new / denom).astype(jnp.bfloat16)
    attended = jnp.einsum("tshl,slhd->tshd", old, vals_h, preferred_element_type=jnp.float32)
    attended = attended + jnp.einsum("tshu,ushd->tshd", new, new_vals, preferred_element_type=jnp.float32)
    attended = attended.reshape(steps * owner_rows, local_width).astype(jnp.bfloat16)
    part = jnp.einsum("rf,fk->kr", attended, w_class, preferred_element_type=jnp.float32)
    classes = part.shape[0]
    packed = jnp.concatenate([part[: classes // 2], part[classes // 2 :]], axis=1)
    packed = jnp.pad(packed, ((0, 1), (0, 0)))
    spread = lax.all_to_all(jnp.broadcast_to(packed[None], (128,) + packed.shape), ("tx", "ty"), 0, 0)
    by_tx = jnp.sum(spread.reshape(8, 16, 8, 128), axis=1)[:, : classes // 2]
    by_tx = by_tx.reshape(8, classes // 2, 2, steps, owner_rows)
    by_slot = by_tx.transpose(2, 1, 3, 0, 4).reshape(classes * steps, total_rows)
    pick = (jnp.arange(total_rows)[:, None] == row_slots[None, :]).astype(jnp.float32)
    logits = jnp.dot(by_slot, pick, precision=lax.Precision.HIGHEST, preferred_element_type=jnp.float32)
    category_logits = logits.reshape(classes, steps, total_rows).transpose(1, 2, 0)
    return (stream_out, category_logits)


def solution(mesh):
    return jax.shard_map(
        per_device,
        mesh=mesh,
        in_specs=(
            P(None, "ty", "tx"),
            P("tx"),
            P("tx", "ty"),
            P("tx", "ty"),
            P("ty", "tx"),
            P("tx", None, "ty"),
            P("ty", None),
            P("tx", None, "ty"),
            P("tx", None, "ty"),
            P("tx"),
            P(),
        ),
        out_specs=(P(None, "ty", "tx"), P()),
        check_vma=False,
    )
```

```python
import functools

import jax
import jax.numpy as jnp
from jax import lax
from jax.experimental import pallas as pl
from jax.experimental.pallas import tpu as pltpu
from jax.sharding import PartitionSpec as P

D = 16384
HEAD_DIM = 128
DOWN = 2.0 ** -24
UP = 2.0 ** 24


def tx_move(array, dy, dz):
    pairs = [(z * 4 + y, (z ^ dz) * 4 + (y + dy) % 4) for z in range(2) for y in range(4)]
    return lax.ppermute(array, "tx", pairs)


def core_swap(array):
    return lax.ppermute(array, "ty", [(n, n ^ 1) for n in range(16)])


def chip_exchange(blocks):
    groups = [[2 * n + c for n in range(8)] for c in range(2)]
    return lax.all_to_all(blocks, "ty", 0, 0, axis_index_groups=groups)


def gather_ty(rows):
    mine = chip_exchange(jnp.broadcast_to(rows[None], (8,) + rows.shape))
    mine = mine.reshape(8 * rows.shape[0], rows.shape[1])
    return mine, core_swap(mine)


def f32(array):
    return array.astype(jnp.float32)


VM = pl.BlockSpec(memory_space=pltpu.VMEM)
ANY = pl.BlockSpec(memory_space=pl.ANY)


def fetch_kernel(source, *refs):
    target, sems = refs[-2:]
    copies = []
    part = source.shape[0] // sems.shape[0]
    for n in range(sems.shape[0]):
        at = pl.ds(n * part, part)
        copies.append(pltpu.make_async_copy(source.at[at], target.at[at], sems.at[n]))
    for copy in copies:
        copy.start()
    for copy in copies:
        copy.wait()


def fetch(array, pieces, *after):
    return pl.pallas_call(
        fetch_kernel,
        out_shape=pltpu.VMEM(array.shape, array.dtype),
        in_specs=[ANY] * (1 + len(after)),
        out_specs=VM,
        scratch_shapes=[pltpu.SemaphoreType.DMA((pieces,))],
        compiler_params=pltpu.CompilerParams(vmem_limit_bytes=2 * 1024 * 1024),
    )(pltpu.with_memory_space_constraint(array, pltpu.HBM), *after)


def scale_rows(order, x_ref, gain_ref, hidden, outs, scaled):
    rows = outs[0].shape[0]
    unit = x_ref.shape[0] // 8
    gain = gain_ref[...].astype(jnp.float32) * DOWN
    lane = lax.broadcasted_iota(jnp.int32, (unit, 128), 1)
    for n in range(8):
        start = pl.multiple_of(order[n] * unit, unit)
        values = x_ref[pl.ds(start, unit), :].astype(jnp.float32)
        scaled[n * unit : (n + 1) * unit, :] = (values * gain).astype(jnp.bfloat16)
        squares = jnp.sum(values * values, axis=1, keepdims=True)
        first = squares.astype(jnp.bfloat16).astype(jnp.float32)
        second = (squares - first).astype(jnp.bfloat16).astype(jnp.float32)
        third = squares - first - second
        columns = jnp.where(lane == 0, first, jnp.where(lane == 1, second, jnp.where(lane == 2, third, 0.0)))
        at = (n * unit) % rows
        outs[n * unit // rows][at : at + unit, 2 * hidden :] = columns.astype(jnp.bfloat16)


def spread(outs, result, start):
    rows = outs[0].shape[0]
    for n, out in enumerate(outs):
        out[:, start : start + result.shape[1]] = result[n * rows : (n + 1) * rows]


def project(scaled, w_ref, outs, base):
    hidden = w_ref.shape[1]
    for start in range(0, hidden, 256):
        stop = min(start + 256, hidden)
        result = jnp.dot(scaled[...], w_ref[:, start:stop], preferred_element_type=jnp.float32)
        spread(outs, result.astype(jnp.bfloat16), base + start)


def load_gate_up_kernel(order, x_ref, gain_ref, wg_hbm, wu_hbm, *refs):
    outs, wg_ref, wu_ref, scaled, half_sum, sems = refs[:-5], *refs[-5:]
    width, hidden = wg_ref.shape
    part = width // 4
    copies = [
        pltpu.make_async_copy(source.at[pl.ds(m * part, part)], target.at[pl.ds(m * part, part)], sems.at[4 * n + m])
        for n, (source, target) in enumerate(((wg_hbm, wg_ref), (wu_hbm, wu_ref)))
        for m in range(4)
    ]
    for copy in copies[:4]:
        copy.start()
    scale_rows(order, x_ref, gain_ref, hidden, outs, scaled)
    for copy in copies[:2]:
        copy.wait()
    for copy in copies[4:]:
        copy.start()
    for start in range(0, hidden, 256):
        stop = min(start + 256, hidden)
        half_sum[:, start:stop] = jnp.dot(
            scaled[:, : 2 * part], wg_ref[: 2 * part, start:stop], preferred_element_type=jnp.float32
        )
    for copy in copies[2:4]:
        copy.wait()
    for start in range(0, hidden, 256):
        stop = min(start + 256, hidden)
        result = half_sum[:, start:stop] + jnp.dot(
            scaled[:, 2 * part :], wg_ref[2 * part :, start:stop], preferred_element_type=jnp.float32
        )
        spread(outs, result.astype(jnp.bfloat16), start)
    for copy in copies[4:]:
        copy.wait()
    project(scaled, wu_ref, outs, hidden)


def gate_up_kernel(order, x_ref, gain_ref, wg_ref, wu_ref, *refs):
    outs, scaled = refs[:-1], refs[-1]
    hidden = wg_ref.shape[1]
    scale_rows(order, x_ref, gain_ref, hidden, outs, scaled)
    project(scaled, wg_ref, outs, 0)
    project(scaled, wu_ref, outs, hidden)


def gate_up(order, x, gain, w_gate, w_up, blocks, load):
    rows, width = x.shape
    hidden = w_gate.shape[1]
    out = jax.ShapeDtypeStruct((rows // blocks, 2 * hidden + 128), jnp.bfloat16)
    scratch = [pltpu.VMEM((rows, width), jnp.bfloat16)]
    held = []
    if load:
        scratch += [pltpu.VMEM((rows, hidden), jnp.float32), pltpu.SemaphoreType.DMA((8,))]
        held = [pltpu.VMEM(w_gate.shape, w_gate.dtype)] * 2
        w_gate = pltpu.with_memory_space_constraint(w_gate, pltpu.HBM)
        w_up = pltpu.with_memory_space_constraint(w_up, pltpu.HBM)
    return pl.pallas_call(
        load_gate_up_kernel if load else gate_up_kernel,
        out_shape=[out] * blocks + held,
        in_specs=[pl.BlockSpec(memory_space=pltpu.SMEM)] + [VM] * 2 + [ANY if load else VM] * 2,
        out_specs=[VM] * (blocks + len(held)),
        scratch_shapes=scratch,
        compiler_params=pltpu.CompilerParams(vmem_limit_bytes=12 * 1024 * 1024),
        cost_estimate=pl.CostEstimate(
            flops=4 * rows * width * hidden, transcendentals=0, bytes_accessed=4 * width * hidden + 4 * rows * hidden
        ),
    )(order, x, gain, w_gate, w_up)


def small_call(kernel, outs, *arrays):
    return pl.pallas_call(
        kernel,
        out_shape=[jax.ShapeDtypeStruct(shape, dtype) for shape, dtype in outs],
        in_specs=[VM] * len(arrays),
        out_specs=[VM] * len(outs),
        compiler_params=pltpu.CompilerParams(vmem_limit_bytes=8 * 1024 * 1024),
    )(*arrays)


def first_sums_kernel(a0, a1, a2, a3, b0, b1, keep_a, go_a, keep_b, go_b1, go_b2, go_b3):
    unit, wide = keep_a.shape
    for start in range(0, wide, 128):
        at = slice(start, start + 128)
        for lo, out in ((0, keep_a), (unit, go_a)):
            rows = slice(lo, lo + unit)
            total = f32(a0[rows, at]) + f32(a1[rows, at]) + f32(a2[rows, at]) + f32(a3[rows, at])
            out[:, at] = total.astype(out.dtype)
        for n, out in enumerate((keep_b, go_b1, go_b2, go_b3)):
            rows = slice(n * unit, (n + 1) * unit)
            out[:, at] = (f32(b0[rows, at]) + f32(b1[rows, at])).astype(out.dtype)


def activate_kernel(keep_a, a1, keep_b, b1, b2, b3, out_a, out_b):
    hidden = out_a.shape[1]
    for keep, others, out in ((keep_a, (a1,), out_a), (keep_b, (b1, b2, b3), out_b)):

        def summed(start):
            at = slice(start, start + 128)
            value = keep[:, at]
            for other in others:
                value = value + f32(other[:, at])
            return value

        squares = jnp.sum(summed(2 * hidden), axis=1, keepdims=True)
        scale = lax.rsqrt(squares / D + 1e-05) * UP
        for start in range(0, hidden, 128):
            gate = summed(start) * scale
            up = summed(hidden + start) * scale
            out[:, start : start + 128] = (gate / (1.0 + jnp.exp(-gate)) * up).astype(jnp.bfloat16)


def stack_kernel(a0, a1, b0, b1, b2, b3, out_a, out_b):
    unit = a0.shape[0]
    for out, parts in ((out_a, (a0, a1)), (out_b, (b0, b1, b2, b3))):
        for n, part in enumerate(parts):
            out[n * unit : (n + 1) * unit, :] = part[...]


def down_kernel(count, order_a, order_b, *refs):
    pieces, w_ref, out_a, out_b, hidden = refs[:-4], *refs[-4:]
    half = hidden.shape[0] // 2
    unit = half // 8
    for base, order, group in ((0, order_a, pieces[:count]), (half, order_b, pieces[count:])):
        per = group[0].shape[0] // unit
        for n in range(8):
            start = pl.multiple_of(order[n] * unit, unit)
            at = (n % per) * unit
            hidden[pl.ds(base + start, unit), :] = group[n // per][at : at + unit, :]
    for start in range(0, w_ref.shape[1], 256):
        result = jnp.dot(hidden[...], w_ref[:, start : start + 256], preferred_element_type=jnp.float32)
        result = result.astype(jnp.bfloat16)
        out_a[:, start : start + 256] = result[:half]
        out_b[:, start : start + 256] = result[half:]


def down(order_a, order_b, pieces_a, pieces_b, w_down):
    rows = sum(piece.shape[0] for piece in pieces_a)
    inner, width = w_down.shape
    pieces = [*pieces_a, *pieces_b]
    return pl.pallas_call(
        functools.partial(down_kernel, len(pieces_a)),
        out_shape=[jax.ShapeDtypeStruct((rows, width), jnp.bfloat16)] * 2,
        in_specs=[pl.BlockSpec(memory_space=pltpu.SMEM)] * 2 + [VM] * (len(pieces) + 1),
        out_specs=[VM] * 2,
        scratch_shapes=[pltpu.VMEM((2 * rows, inner), jnp.bfloat16)],
        compiler_params=pltpu.CompilerParams(vmem_limit_bytes=10 * 1024 * 1024),
    )(order_a, order_b, *pieces, w_down)


def qkv_kernel(mine_ref, other_ref, src_ref, dst_ref, w_ref, out, ordered):
    half = mine_ref.shape[0]
    pick = jnp.where(dst_ref[...] == src_ref[...], 1.0, 0.0).astype(jnp.bfloat16)
    for start in range(0, mine_ref.shape[1], 512):
        at = slice(start, start + 512)
        rows = jnp.dot(pick[:, :half], mine_ref[:, at], preferred_element_type=jnp.float32)
        rows = rows + jnp.dot(pick[:, half:], other_ref[:, at], preferred_element_type=jnp.float32)
        ordered[:, at] = rows.astype(jnp.bfloat16)
    wide = w_ref.shape[2]
    for part in range(w_ref.shape[0]):
        result = jnp.dot(ordered[...], w_ref[part], preferred_element_type=jnp.float32).astype(jnp.bfloat16)
        out[:, part * wide : (part + 1) * wide] = result


def slot_qkv(mine, other, key_src, key_dst, w_parts):
    half, width = mine.shape
    rows = 2 * half
    parts, _, wide = w_parts.shape
    return pl.pallas_call(
        qkv_kernel,
        out_shape=jax.ShapeDtypeStruct((rows, parts * wide), jnp.bfloat16),
        in_specs=[VM] * 5,
        out_specs=VM,
        scratch_shapes=[pltpu.VMEM((rows, width), jnp.bfloat16)],
        compiler_params=pltpu.CompilerParams(vmem_limit_bytes=12 * 1024 * 1024),
        cost_estimate=pl.CostEstimate(
            flops=2 * rows * width * (parts * wide + rows),
            transcendentals=0,
            bytes_accessed=2 * width * (parts * wide + rows),
        ),
    )(mine, other, key_src, key_dst, w_parts)


def per_device(
    states,
    norm_gain,
    w_gate,
    w_up,
    w_down,
    w_qkv,
    w_class,
    cache_keys,
    cache_values,
    cache_lengths,
    row_slots,
):
    steps = states.shape[0]
    local_rows = states.shape[1]
    width = states.shape[2]
    hidden_here = w_gate.shape[1]
    owner_rows = cache_keys.shape[0]
    history = cache_keys.shape[1]
    local_width = w_qkv.shape[2]
    heads_here = local_width // HEAD_DIM
    total_rows = row_slots.shape[0]
    rows = steps * total_rows
    per = steps * local_rows
    block = rows // 8
    unit = block // 2
    tx = lax.axis_index("tx")
    ty = lax.axis_index("ty")
    my_y, my_zh = tx % 4, tx // 4

    def to(dy, dz):
        return (my_zh ^ dz) * 4 + (my_y + dy) % 4

    def source(dy, dz):
        return (my_zh ^ dz) * 4 + (my_y - dy + 4) % 4

    y_major = [(dy, dz) for dy in range(4) for dz in range(2)]
    z_major = [(dy, dz) for dz in range(2) for dy in range(4)]
    send_a = jnp.stack([to(*m) for m in y_major])
    send_b = jnp.stack([to(*m) for m in z_major])
    from_a = jnp.stack([source(*m) for m in y_major])
    from_b = jnp.stack([source(*m) for m in z_major])

    pos = jnp.arange(rows, dtype=jnp.int32)
    chunk = pos // per
    source_ty = 2 * (chunk % 8) + ((ty % 2) ^ (chunk // 8))
    row_of = source_ty * local_rows + pos % local_rows
    hit = row_of[:, None] == jnp.arange(total_rows, dtype=jnp.int32)[None, :]
    slot_of = jnp.sum(jnp.where(hit, row_slots[None, :], 0), axis=1)
    key_src = (((pos % per) // local_rows) * total_rows + slot_of)[None, :]
    key_dst = ((pos % block) // owner_rows) * total_rows + pos // block * owner_rows + pos % owner_rows
    key_dst = key_dst[:, None]

    own = states.reshape(per, width)
    gain = norm_gain[None, :]
    mine, other = gather_ty(own)
    *part_a, w_gate, w_up = gate_up(send_a, mine, gain, w_gate, w_up, 4, True)
    part_b = gate_up(send_b, other, gain, w_gate, w_up, 2, False)
    half_send = (unit, part_a[0].shape[1])
    came_a = [tx_move(part_a[dy], dy, 0) for dy in (2, 1, 3)]
    came_b = tx_move(part_b[1], 0, 1)
    keep_a, go_a, keep_b, *go_b = small_call(
        first_sums_kernel,
        [(half_send, jnp.float32), (half_send, jnp.bfloat16), (half_send, jnp.float32)] + [(half_send, jnp.bfloat16)] * 3,
        part_a[0], *came_a, part_b[0], came_b,
    )
    came_b = [tx_move(go_b[dy - 1], dy, 0) for dy in (2, 1, 3)]
    came_a = tx_move(go_a, 0, 1)
    half_hidden = ((unit, hidden_here), jnp.bfloat16)
    hidden_a, hidden_b = small_call(activate_kernel, [half_hidden] * 2, keep_a, came_a, keep_b, *came_b)
    came_b = [tx_move(hidden_b, dy, 0) for dy in (1, 2, 3)]
    came_a = tx_move(hidden_a, 0, 1)
    pair_a, line_b = small_call(
        stack_kernel,
        [((2 * unit, hidden_here), jnp.bfloat16), ((4 * unit, hidden_here), jnp.bfloat16)],
        hidden_a, came_a, hidden_b, *came_b,
    )
    pieces_a = [pair_a] + [tx_move(pair_a, dy, 0) for dy in (1, 2, 3)]
    pieces_b = [line_b, tx_move(line_b, 0, 1)]
    w_down = fetch(w_down, 4, pair_a)
    mixed_a, mixed_b = down(from_a, from_b, pieces_a, pieces_b, w_down)
    chip = (f32(mixed_a) + f32(core_swap(mixed_b))).astype(jnp.bfloat16)
    parts = chip_exchange(chip.reshape(8, per, width))
    stream = (f32(own) + jnp.sum(f32(parts), axis=0)).astype(jnp.bfloat16)
    stream_out = stream.reshape(steps, local_rows, width)

    mine, other = gather_ty(stream)
    w_parts = fetch(jnp.transpose(w_qkv, (1, 0, 2)), 3, mine)
    qkv = slot_qkv(mine, other, key_src, key_dst, w_parts)
    received = lax.all_to_all(qkv.reshape(8, block, 3 * local_width), "tx", 0, 0)
    triple = jnp.sum(f32(received), axis=0).astype(jnp.bfloat16)
    triple = triple.reshape(steps, owner_rows, 3, heads_here, HEAD_DIM)
    query, new_keys, new_vals = triple[:, :, 0], triple[:, :, 1], triple[:, :, 2]
    keys_h = cache_keys.reshape(owner_rows, history, heads_here, HEAD_DIM)
    vals_h = cache_values.reshape(owner_rows, history, heads_here, HEAD_DIM)
    old = jnp.einsum("tshd,slhd->tshl", query, keys_h, preferred_element_type=jnp.float32)
    new = jnp.einsum("tshd,ushd->tshu", query, new_keys, preferred_element_type=jnp.float32)
    old = old * HEAD_DIM ** (-0.5)
    new = new * HEAD_DIM ** (-0.5)
    where_pos = jnp.arange(history, dtype=jnp.int32)
    old = jnp.where((where_pos[None, :] < cache_lengths[:, None])[None, :, None, :], old, jnp.float32(-1e30))
    causal = jnp.arange(steps)[:, None] >= jnp.arange(steps)[None, :]
    new = jnp.where(causal[:, None, None, :], new, jnp.float32(-1e30))
    top = jnp.maximum(jnp.max(old, axis=3, keepdims=True), jnp.max(new, axis=3, keepdims=True))
    old = jnp.exp(old - top)
    new = jnp.exp(new - top)
    denom = jnp.sum(old, axis=3, keepdims=True) + jnp.sum(new, axis=3, keepdims=True)
    old = (old / denom).astype(jnp.bfloat16)
    new = (new / denom).astype(jnp.bfloat16)
    attended = jnp.einsum("tshl,slhd->tshd", old, vals_h, preferred_element_type=jnp.float32)
    attended = attended + jnp.einsum("tshu,ushd->tshd", new, new_vals, preferred_element_type=jnp.float32)
    attended = attended.reshape(steps * owner_rows, local_width).astype(jnp.bfloat16)
    part = jnp.einsum("rf,fk->kr", attended, w_class, preferred_element_type=jnp.float32)
    classes = part.shape[0]
    packed = jnp.concatenate([part[: classes // 2], part[classes // 2 :]], axis=1)
    packed = jnp.pad(packed, ((0, 1), (0, 0)))
    spread = lax.all_to_all(jnp.broadcast_to(packed[None], (128,) + packed.shape), ("tx", "ty"), 0, 0)
    by_tx = jnp.sum(spread.reshape(8, 16, 8, 128), axis=1)[:, : classes // 2]
    by_tx = by_tx.reshape(8, classes // 2, 2, steps, owner_rows)
    by_slot = by_tx.transpose(2, 1, 3, 0, 4).reshape(classes * steps, total_rows)
    pick = (jnp.arange(total_rows)[:, None] == row_slots[None, :]).astype(jnp.float32)
    logits = jnp.dot(by_slot, pick, precision=lax.Precision.HIGHEST, preferred_element_type=jnp.float32)
    category_logits = logits.reshape(classes, steps, total_rows).transpose(1, 2, 0)
    return (stream_out, category_logits)


def solution(mesh):
    return jax.shard_map(
        per_device,
        mesh=mesh,
        in_specs=(
            P(None, "ty", "tx"),
            P("tx"),
            P("tx", "ty"),
            P("tx", "ty"),
            P("ty", "tx"),
            P("tx", None, "ty"),
            P("ty", None),
            P("tx", None, "ty"),
            P("tx", None, "ty"),
            P("tx"),
            P(),
        ),
        out_specs=(P(None, "ty", "tx"), P()),
        check_vma=False,
    )
```

```python
import functools

import jax
import jax.numpy as jnp
from jax import lax
from jax.experimental import pallas as pl
from jax.experimental.pallas import tpu as pltpu
from jax.sharding import PartitionSpec as P

D = 16384
HEAD_DIM = 128
DOWN = 2.0 ** -24
UP = 2.0 ** 24


def tx_move(array, dy, dz):
    pairs = [(z * 4 + y, (z ^ dz) * 4 + (y + dy) % 4) for z in range(2) for y in range(4)]
    return lax.ppermute(array, "tx", pairs)


def core_swap(array):
    return lax.ppermute(array, "ty", [(n, n ^ 1) for n in range(16)])


def chip_exchange(blocks):
    groups = [[2 * n + c for n in range(8)] for c in range(2)]
    return lax.all_to_all(blocks, "ty", 0, 0, axis_index_groups=groups)


def gather_ty(rows):
    mine = chip_exchange(jnp.broadcast_to(rows[None], (8,) + rows.shape))
    mine = mine.reshape(8 * rows.shape[0], rows.shape[1])
    return mine, core_swap(mine)


def f32(array):
    return array.astype(jnp.float32)


VM = pl.BlockSpec(memory_space=pltpu.VMEM)
ANY = pl.BlockSpec(memory_space=pl.ANY)


def fetch_kernel(source, *refs):
    target, sems = refs[-2:]
    copies = []
    part = source.shape[0] // sems.shape[0]
    for n in range(sems.shape[0]):
        at = pl.ds(n * part, part)
        copies.append(pltpu.make_async_copy(source.at[at], target.at[at], sems.at[n]))
    for copy in copies:
        copy.start()
    for copy in copies:
        copy.wait()


def fetch(array, pieces, *after):
    return pl.pallas_call(
        fetch_kernel,
        out_shape=pltpu.VMEM(array.shape, array.dtype),
        in_specs=[ANY] * (1 + len(after)),
        out_specs=VM,
        scratch_shapes=[pltpu.SemaphoreType.DMA((pieces,))],
        compiler_params=pltpu.CompilerParams(vmem_limit_bytes=2 * 1024 * 1024),
    )(pltpu.with_memory_space_constraint(array, pltpu.HBM), *after)


def scale_rows(order, x_ref, gain_ref, hidden, outs, scaled):
    rows = outs[0].shape[0]
    unit = x_ref.shape[0] // 8
    gain = gain_ref[...].astype(jnp.float32) * DOWN
    lane = lax.broadcasted_iota(jnp.int32, (unit, 128), 1)
    for n in range(8):
        start = pl.multiple_of(order[n] * unit, unit)
        values = x_ref[pl.ds(start, unit), :].astype(jnp.float32)
        scaled[n * unit : (n + 1) * unit, :] = (values * gain).astype(jnp.bfloat16)
        squares = jnp.sum(values * values, axis=1, keepdims=True)
        first = squares.astype(jnp.bfloat16).astype(jnp.float32)
        second = (squares - first).astype(jnp.bfloat16).astype(jnp.float32)
        third = squares - first - second
        columns = jnp.where(lane == 0, first, jnp.where(lane == 1, second, jnp.where(lane == 2, third, 0.0)))
        at = (n * unit) % rows
        outs[n * unit // rows][at : at + unit, 2 * hidden :] = columns.astype(jnp.bfloat16)


def spread(outs, result, start):
    rows = outs[0].shape[0]
    for n, out in enumerate(outs):
        out[:, start : start + result.shape[1]] = result[n * rows : (n + 1) * rows]


def project(scaled, w_ref, outs, base):
    hidden = w_ref.shape[1]
    for start in range(0, hidden, 256):
        stop = min(start + 256, hidden)
        result = jnp.dot(scaled[...], w_ref[:, start:stop], preferred_element_type=jnp.float32)
        spread(outs, result.astype(jnp.bfloat16), base + start)


def load_gate_up_kernel(order, x_ref, gain_ref, wg_hbm, wu_hbm, *refs):
    outs, wg_ref, wu_ref, scaled, half_sum, sems = refs[:-5], *refs[-5:]
    width, hidden = wg_ref.shape
    part = width // 4
    copies = [
        pltpu.make_async_copy(source.at[pl.ds(m * part, part)], target.at[pl.ds(m * part, part)], sems.at[4 * n + m])
        for n, (source, target) in enumerate(((wg_hbm, wg_ref), (wu_hbm, wu_ref)))
        for m in range(4)
    ]
    for copy in copies[:4]:
        copy.start()
    scale_rows(order, x_ref, gain_ref, hidden, outs, scaled)
    for copy in copies[:2]:
        copy.wait()
    for copy in copies[4:]:
        copy.start()
    for start in range(0, hidden, 256):
        stop = min(start + 256, hidden)
        half_sum[:, start:stop] = jnp.dot(
            scaled[:, : 2 * part], wg_ref[: 2 * part, start:stop], preferred_element_type=jnp.float32
        )
    for copy in copies[2:4]:
        copy.wait()
    for start in range(0, hidden, 256):
        stop = min(start + 256, hidden)
        result = half_sum[:, start:stop] + jnp.dot(
            scaled[:, 2 * part :], wg_ref[2 * part :, start:stop], preferred_element_type=jnp.float32
        )
        spread(outs, result.astype(jnp.bfloat16), start)
    for copy in copies[4:]:
        copy.wait()
    project(scaled, wu_ref, outs, hidden)


def gate_up_kernel(order, x_ref, gain_ref, wg_ref, wu_ref, *refs):
    outs, scaled = refs[:-1], refs[-1]
    hidden = wg_ref.shape[1]
    scale_rows(order, x_ref, gain_ref, hidden, outs, scaled)
    project(scaled, wg_ref, outs, 0)
    project(scaled, wu_ref, outs, hidden)


def gate_up(order, x, gain, w_gate, w_up, blocks, load):
    rows, width = x.shape
    hidden = w_gate.shape[1]
    out = jax.ShapeDtypeStruct((rows // blocks, 2 * hidden + 128), jnp.bfloat16)
    scratch = [pltpu.VMEM((rows, width), jnp.bfloat16)]
    held = []
    if load:
        scratch += [pltpu.VMEM((rows, hidden), jnp.float32), pltpu.SemaphoreType.DMA((8,))]
        held = [pltpu.VMEM(w_gate.shape, w_gate.dtype)] * 2
        w_gate = pltpu.with_memory_space_constraint(w_gate, pltpu.HBM)
        w_up = pltpu.with_memory_space_constraint(w_up, pltpu.HBM)
    return pl.pallas_call(
        load_gate_up_kernel if load else gate_up_kernel,
        out_shape=[out] * blocks + held,
        in_specs=[pl.BlockSpec(memory_space=pltpu.SMEM)] + [VM] * 2 + [ANY if load else VM] * 2,
        out_specs=[VM] * (blocks + len(held)),
        scratch_shapes=scratch,
        compiler_params=pltpu.CompilerParams(vmem_limit_bytes=12 * 1024 * 1024),
        cost_estimate=pl.CostEstimate(
            flops=4 * rows * width * hidden, transcendentals=0, bytes_accessed=4 * width * hidden + 4 * rows * hidden
        ),
    )(order, x, gain, w_gate, w_up)


def small_call(kernel, outs, *arrays):
    return pl.pallas_call(
        kernel,
        out_shape=[jax.ShapeDtypeStruct(shape, dtype) for shape, dtype in outs],
        in_specs=[VM] * len(arrays),
        out_specs=[VM] * len(outs),
        compiler_params=pltpu.CompilerParams(vmem_limit_bytes=8 * 1024 * 1024),
    )(*arrays)


def first_sums_kernel(a0, a1, a2, a3, b0, b1, c0, c1, keep_a, go_a, keep_b, go_b1, go_b2, go_b3):
    unit, wide = keep_a.shape
    for start in range(0, wide, 128):
        at = slice(start, start + 128)
        for lo, out in ((0, keep_a), (unit, go_a)):
            rows = slice(lo, lo + unit)
            total = f32(a0[rows, at]) + f32(a1[rows, at]) + f32(a2[rows, at]) + f32(a3[rows, at])
            out[:, at] = total.astype(out.dtype)
        for n, out in enumerate((keep_b, go_b1, go_b2, go_b3)):
            rows = slice((n % 2) * unit, (n % 2 + 1) * unit)
            own, came = (b0, c0) if n < 2 else (b1, c1)
            out[:, at] = (f32(own[rows, at]) + f32(came[rows, at])).astype(out.dtype)


def activate_kernel(keep_a, a1, keep_b, b1, b2, b3, out_a, out_b):
    hidden = out_a.shape[1]
    for keep, others, out in ((keep_a, (a1,), out_a), (keep_b, (b1, b2, b3), out_b)):

        def summed(start):
            at = slice(start, start + 128)
            value = keep[:, at]
            for other in others:
                value = value + f32(other[:, at])
            return value

        squares = jnp.sum(summed(2 * hidden), axis=1, keepdims=True)
        scale = lax.rsqrt(squares / D + 1e-05) * UP
        for start in range(0, hidden, 128):
            gate = summed(start) * scale
            up = summed(hidden + start) * scale
            out[:, start : start + 128] = (gate / (1.0 + jnp.exp(-gate)) * up).astype(jnp.bfloat16)


def stack_kernel(a0, a1, b0, b1, b2, b3, out_a, out_b):
    unit = a0.shape[0]
    for out, parts in ((out_a, (a0, a1)), (out_b, (b0, b1, b2, b3))):
        for n, part in enumerate(parts):
            out[n * unit : (n + 1) * unit, :] = part[...]


def down_kernel(count, order_a, order_b, *refs):
    pieces, w_ref, out_a, out_b, hidden = refs[:-4], *refs[-4:]
    half = hidden.shape[0] // 2
    unit = half // 8
    for base, order, group in ((0, order_a, pieces[:count]), (half, order_b, pieces[count:])):
        per = group[0].shape[0] // unit
        for n in range(8):
            start = pl.multiple_of(order[n] * unit, unit)
            at = (n % per) * unit
            hidden[pl.ds(base + start, unit), :] = group[n // per][at : at + unit, :]
    for start in range(0, w_ref.shape[1], 256):
        result = jnp.dot(hidden[...], w_ref[:, start : start + 256], preferred_element_type=jnp.float32)
        result = result.astype(jnp.bfloat16)
        out_a[:, start : start + 256] = result[:half]
        out_b[:, start : start + 256] = result[half:]


def down(order_a, order_b, pieces_a, pieces_b, w_down):
    rows = sum(piece.shape[0] for piece in pieces_a)
    inner, width = w_down.shape
    pieces = [*pieces_a, *pieces_b]
    return pl.pallas_call(
        functools.partial(down_kernel, len(pieces_a)),
        out_shape=[jax.ShapeDtypeStruct((rows, width), jnp.bfloat16)] * 2,
        in_specs=[pl.BlockSpec(memory_space=pltpu.SMEM)] * 2 + [VM] * (len(pieces) + 1),
        out_specs=[VM] * 2,
        scratch_shapes=[pltpu.VMEM((2 * rows, inner), jnp.bfloat16)],
        compiler_params=pltpu.CompilerParams(vmem_limit_bytes=10 * 1024 * 1024),
    )(order_a, order_b, *pieces, w_down)


def qkv_kernel(mine_ref, other_ref, src_ref, dst_ref, w_ref, *refs):
    outs, ordered = refs[:-1], refs[-1]
    half = mine_ref.shape[0]
    pick = jnp.where(dst_ref[...] == src_ref[...], 1.0, 0.0).astype(jnp.bfloat16)
    for start in range(0, mine_ref.shape[1], 512):
        at = slice(start, start + 512)
        rows = jnp.dot(pick[:, :half], mine_ref[:, at], preferred_element_type=jnp.float32)
        rows = rows + jnp.dot(pick[:, half:], other_ref[:, at], preferred_element_type=jnp.float32)
        ordered[:, at] = rows.astype(jnp.bfloat16)
    wide = w_ref.shape[2]
    for part in range(w_ref.shape[0]):
        result = jnp.dot(ordered[...], w_ref[part], preferred_element_type=jnp.float32).astype(jnp.bfloat16)
        spread(outs, result, part * wide)


def slot_qkv(mine, other, key_src, key_dst, w_parts):
    half, width = mine.shape
    rows = 2 * half
    parts, _, wide = w_parts.shape
    return pl.pallas_call(
        qkv_kernel,
        out_shape=[jax.ShapeDtypeStruct((rows // 8, parts * wide), jnp.bfloat16)] * 8,
        in_specs=[VM] * 5,
        out_specs=[VM] * 8,
        scratch_shapes=[pltpu.VMEM((rows, width), jnp.bfloat16)],
        compiler_params=pltpu.CompilerParams(vmem_limit_bytes=12 * 1024 * 1024),
        cost_estimate=pl.CostEstimate(
            flops=2 * rows * width * (parts * wide + rows),
            transcendentals=0,
            bytes_accessed=2 * width * (parts * wide + rows),
        ),
    )(mine, other, key_src, key_dst, w_parts)


def per_device(
    states,
    norm_gain,
    w_gate,
    w_up,
    w_down,
    w_qkv,
    w_class,
    cache_keys,
    cache_values,
    cache_lengths,
    row_slots,
):
    steps = states.shape[0]
    local_rows = states.shape[1]
    width = states.shape[2]
    hidden_here = w_gate.shape[1]
    owner_rows = cache_keys.shape[0]
    history = cache_keys.shape[1]
    local_width = w_qkv.shape[2]
    heads_here = local_width // HEAD_DIM
    total_rows = row_slots.shape[0]
    rows = steps * total_rows
    per = steps * local_rows
    block = rows // 8
    unit = block // 2
    tx = lax.axis_index("tx")
    ty = lax.axis_index("ty")
    my_y, my_zh = tx % 4, tx // 4

    def to(dy, dz):
        return (my_zh ^ dz) * 4 + (my_y + dy) % 4

    def source(dy, dz):
        return (my_zh ^ dz) * 4 + (my_y - dy + 4) % 4

    y_major = [(dy, dz) for dy in range(4) for dz in range(2)]
    z_major = [(dy, dz) for dz in range(2) for dy in range(4)]
    send_a = jnp.stack([to(*m) for m in y_major])
    send_b = jnp.stack([to(*m) for m in z_major])
    from_a = jnp.stack([source(*m) for m in y_major])
    from_b = jnp.stack([source(*m) for m in z_major])

    pos = jnp.arange(rows, dtype=jnp.int32)
    chunk = pos // per
    source_ty = 2 * (chunk % 8) + ((ty % 2) ^ (chunk // 8))
    row_of = source_ty * local_rows + pos % local_rows
    hit = row_of[:, None] == jnp.arange(total_rows, dtype=jnp.int32)[None, :]
    slot_of = jnp.sum(jnp.where(hit, row_slots[None, :], 0), axis=1)
    key_src = (((pos % per) // local_rows) * total_rows + slot_of)[None, :]
    moves = [(0, 0), (2, 1), (1, 1), (3, 1), (2, 0), (0, 1), (1, 0), (3, 0)]
    target = jnp.zeros((rows,), jnp.int32)
    for n, move in enumerate(moves):
        target = jnp.where(pos // block == n, to(*move), target)
    key_dst = ((pos % block) // owner_rows) * total_rows + target * owner_rows + pos % owner_rows
    key_dst = key_dst[:, None]

    own = states.reshape(per, width)
    gain = norm_gain[None, :]
    mine, other = gather_ty(own)
    *part_a, w_gate, w_up = gate_up(send_a, mine, gain, w_gate, w_up, 4, True)
    part_b = gate_up(send_b, other, gain, w_gate, w_up, 4, False)
    half_send = (unit, part_a[0].shape[1])
    came_a = [tx_move(part_a[dy], dy, 0) for dy in (2, 1, 3)]
    came_b = [tx_move(part_b[n], 0, 1) for n in (2, 3)]
    keep_a, go_a, keep_b, *go_b = small_call(
        first_sums_kernel,
        [(half_send, jnp.float32), (half_send, jnp.bfloat16), (half_send, jnp.float32)] + [(half_send, jnp.bfloat16)] * 3,
        part_a[0], *came_a, *part_b[:2], *came_b,
    )
    came_b = [tx_move(go_b[dy - 1], dy, 0) for dy in (2, 1, 3)]
    came_a = tx_move(go_a, 0, 1)
    half_hidden = ((unit, hidden_here), jnp.bfloat16)
    hidden_a, hidden_b = small_call(activate_kernel, [half_hidden] * 2, keep_a, came_a, keep_b, *came_b)
    came_b = [tx_move(hidden_b, dy, 0) for dy in (1, 2, 3)]
    came_a = tx_move(hidden_a, 0, 1)
    pair_a, line_b = small_call(
        stack_kernel,
        [((2 * unit, hidden_here), jnp.bfloat16), ((4 * unit, hidden_here), jnp.bfloat16)],
        hidden_a, came_a, hidden_b, *came_b,
    )
    pieces_a = [pair_a] + [tx_move(pair_a, dy, 0) for dy in (1, 2, 3)]
    pieces_b = [line_b, tx_move(line_b, 0, 1)]
    w_down = fetch(w_down, 4, pair_a)
    mixed_a, mixed_b = down(from_a, from_b, pieces_a, pieces_b, w_down)
    chip = (f32(mixed_a) + f32(core_swap(mixed_b))).astype(jnp.bfloat16)
    parts = chip_exchange(chip.reshape(8, per, width))
    stream = (f32(own) + jnp.sum(f32(parts), axis=0)).astype(jnp.bfloat16)
    stream_out = stream.reshape(steps, local_rows, width)

    mine, other = gather_ty(stream)
    w_parts = fetch(jnp.transpose(w_qkv, (1, 0, 2)), 3, mine)
    qkv = slot_qkv(mine, other, key_src, key_dst, w_parts)
    triple = f32(qkv[0])
    for piece, move in zip(qkv[1:], moves[1:]):
        triple = triple + f32(tx_move(piece, *move))
    triple = triple.astype(jnp.bfloat16)
    triple = triple.reshape(steps, owner_rows, 3, heads_here, HEAD_DIM)
    query, new_keys, new_vals = triple[:, :, 0], triple[:, :, 1], triple[:, :, 2]
    keys_h = cache_keys.reshape(owner_rows, history, heads_here, HEAD_DIM)
    vals_h = cache_values.reshape(owner_rows, history, heads_here, HEAD_DIM)
    old = jnp.einsum("tshd,slhd->tshl", query, keys_h, preferred_element_type=jnp.float32)
    new = jnp.einsum("tshd,ushd->tshu", query, new_keys, preferred_element_type=jnp.float32)
    old = old * HEAD_DIM ** (-0.5)
    new = new * HEAD_DIM ** (-0.5)
    where_pos = jnp.arange(history, dtype=jnp.int32)
    old = jnp.where((where_pos[None, :] < cache_lengths[:, None])[None, :, None, :], old, jnp.float32(-1e30))
    causal = jnp.arange(steps)[:, None] >= jnp.arange(steps)[None, :]
    new = jnp.where(causal[:, None, None, :], new, jnp.float32(-1e30))
    top = jnp.maximum(jnp.max(old, axis=3, keepdims=True), jnp.max(new, axis=3, keepdims=True))
    old = jnp.exp(old - top)
    new = jnp.exp(new - top)
    denom = jnp.sum(old, axis=3, keepdims=True) + jnp.sum(new, axis=3, keepdims=True)
    old = (old / denom).astype(jnp.bfloat16)
    new = (new / denom).astype(jnp.bfloat16)
    attended = jnp.einsum("tshl,slhd->tshd", old, vals_h, preferred_element_type=jnp.float32)
    attended = attended + jnp.einsum("tshu,ushd->tshd", new, new_vals, preferred_element_type=jnp.float32)
    attended = attended.reshape(steps * owner_rows, local_width).astype(jnp.bfloat16)
    part = jnp.einsum("rf,fk->kr", attended, w_class, preferred_element_type=jnp.float32)
    classes = part.shape[0]
    packed = jnp.concatenate([part[: classes // 2], part[classes // 2 :]], axis=1)
    packed = jnp.pad(packed, ((0, 1), (0, 0)))
    spread = lax.all_to_all(jnp.broadcast_to(packed[None], (128,) + packed.shape), ("tx", "ty"), 0, 0)
    by_tx = jnp.sum(spread.reshape(8, 16, 8, 128), axis=1)[:, : classes // 2]
    by_tx = by_tx.reshape(8, classes // 2, 2, steps, owner_rows)
    by_slot = by_tx.transpose(2, 1, 3, 0, 4).reshape(classes * steps, total_rows)
    pick = (jnp.arange(total_rows)[:, None] == row_slots[None, :]).astype(jnp.float32)
    logits = jnp.dot(by_slot, pick, precision=lax.Precision.HIGHEST, preferred_element_type=jnp.float32)
    category_logits = logits.reshape(classes, steps, total_rows).transpose(1, 2, 0)
    return (stream_out, category_logits)


def solution(mesh):
    return jax.shard_map(
        per_device,
        mesh=mesh,
        in_specs=(
            P(None, "ty", "tx"),
            P("tx"),
            P("tx", "ty"),
            P("tx", "ty"),
            P("ty", "tx"),
            P("tx", None, "ty"),
            P("ty", None),
            P("tx", None, "ty"),
            P("tx", None, "ty"),
            P("tx"),
            P(),
        ),
        out_specs=(P(None, "ty", "tx"), P()),
        check_vma=False,
    )
```

```python
import functools

import jax
import jax.numpy as jnp
from jax import lax
from jax.experimental import pallas as pl
from jax.experimental.pallas import tpu as pltpu
from jax.sharding import PartitionSpec as P

D = 16384
HEAD_DIM = 128
DOWN = 2.0 ** -24
UP = 2.0 ** 24


def tx_move(array, dy, dz):
    pairs = [(z * 4 + y, (z ^ dz) * 4 + (y + dy) % 4) for z in range(2) for y in range(4)]
    return lax.ppermute(array, "tx", pairs)


def core_swap(array):
    return lax.ppermute(array, "ty", [(n, n ^ 1) for n in range(16)])


def chip_exchange(blocks):
    groups = [[2 * n + c for n in range(8)] for c in range(2)]
    return lax.all_to_all(blocks, "ty", 0, 0, axis_index_groups=groups)


def gather_ty(rows):
    mine = chip_exchange(jnp.broadcast_to(rows[None], (8,) + rows.shape))
    mine = mine.reshape(8 * rows.shape[0], rows.shape[1])
    return mine, core_swap(mine)


def f32(array):
    return array.astype(jnp.float32)


VM = pl.BlockSpec(memory_space=pltpu.VMEM)
ANY = pl.BlockSpec(memory_space=pl.ANY)


def fetch_kernel(source, *refs):
    target, sems = refs[-2:]
    copies = []
    part = source.shape[0] // sems.shape[0]
    for n in range(sems.shape[0]):
        at = pl.ds(n * part, part)
        copies.append(pltpu.make_async_copy(source.at[at], target.at[at], sems.at[n]))
    for copy in copies:
        copy.start()
    for copy in copies:
        copy.wait()


def fetch(array, pieces, *after):
    return pl.pallas_call(
        fetch_kernel,
        out_shape=pltpu.VMEM(array.shape, array.dtype),
        in_specs=[ANY] * (1 + len(after)),
        out_specs=VM,
        scratch_shapes=[pltpu.SemaphoreType.DMA((pieces,))],
        compiler_params=pltpu.CompilerParams(vmem_limit_bytes=2 * 1024 * 1024),
    )(pltpu.with_memory_space_constraint(array, pltpu.HBM), *after)


def scale_rows(order, x_ref, gain_ref, hidden, outs, scaled):
    rows = outs[0].shape[0]
    unit = x_ref.shape[0] // 8
    gain = gain_ref[...].astype(jnp.float32) * DOWN
    lane = lax.broadcasted_iota(jnp.int32, (unit, 128), 1)
    for n in range(8):
        start = pl.multiple_of(order[n] * unit, unit)
        values = x_ref[pl.ds(start, unit), :].astype(jnp.float32)
        scaled[n * unit : (n + 1) * unit, :] = (values * gain).astype(jnp.bfloat16)
        squares = jnp.sum(values * values, axis=1, keepdims=True)
        first = squares.astype(jnp.bfloat16).astype(jnp.float32)
        second = (squares - first).astype(jnp.bfloat16).astype(jnp.float32)
        third = squares - first - second
        columns = jnp.where(lane == 0, first, jnp.where(lane == 1, second, jnp.where(lane == 2, third, 0.0)))
        at = (n * unit) % rows
        outs[n * unit // rows][at : at + unit, 2 * hidden :] = columns.astype(jnp.bfloat16)


def spread(outs, result, start):
    rows = outs[0].shape[0]
    for n, out in enumerate(outs):
        out[:, start : start + result.shape[1]] = result[n * rows : (n + 1) * rows]


def project(scaled, w_ref, outs, base):
    hidden = w_ref.shape[1]
    for start in range(0, hidden, 256):
        stop = min(start + 256, hidden)
        result = jnp.dot(scaled[...], w_ref[:, start:stop], preferred_element_type=jnp.float32)
        spread(outs, result.astype(jnp.bfloat16), base + start)


def load_gate_up_kernel(order, x_ref, gain_ref, wg_hbm, wu_hbm, *refs):
    outs, wg_ref, wu_ref, scaled, half_sum, sems = refs[:-5], *refs[-5:]
    width, hidden = wg_ref.shape
    part = width // 4
    copies = [
        pltpu.make_async_copy(source.at[pl.ds(m * part, part)], target.at[pl.ds(m * part, part)], sems.at[4 * n + m])
        for n, (source, target) in enumerate(((wg_hbm, wg_ref), (wu_hbm, wu_ref)))
        for m in range(4)
    ]
    for copy in copies[:4]:
        copy.start()
    scale_rows(order, x_ref, gain_ref, hidden, outs, scaled)
    for copy in copies[:2]:
        copy.wait()
    for copy in copies[4:]:
        copy.start()
    for start in range(0, hidden, 256):
        stop = min(start + 256, hidden)
        half_sum[:, start:stop] = jnp.dot(
            scaled[:, : 2 * part], wg_ref[: 2 * part, start:stop], preferred_element_type=jnp.float32
        )
    for copy in copies[2:4]:
        copy.wait()
    for start in range(0, hidden, 256):
        stop = min(start + 256, hidden)
        result = half_sum[:, start:stop] + jnp.dot(
            scaled[:, 2 * part :], wg_ref[2 * part :, start:stop], preferred_element_type=jnp.float32
        )
        spread(outs, result.astype(jnp.bfloat16), start)
    for copy in copies[4:]:
        copy.wait()
    project(scaled, wu_ref, outs, hidden)


def gate_up_kernel(order, x_ref, gain_ref, wg_ref, wu_ref, *refs):
    outs, scaled = refs[:-1], refs[-1]
    hidden = wg_ref.shape[1]
    scale_rows(order, x_ref, gain_ref, hidden, outs, scaled)
    project(scaled, wg_ref, outs, 0)
    project(scaled, wu_ref, outs, hidden)


def gate_up(order, x, gain, w_gate, w_up, blocks, load):
    rows, width = x.shape
    hidden = w_gate.shape[1]
    out = jax.ShapeDtypeStruct((rows // blocks, 2 * hidden + 128), jnp.bfloat16)
    scratch = [pltpu.VMEM((rows, width), jnp.bfloat16)]
    held = []
    if load:
        scratch += [pltpu.VMEM((rows, hidden), jnp.float32), pltpu.SemaphoreType.DMA((8,))]
        held = [pltpu.VMEM(w_gate.shape, w_gate.dtype)] * 2
        w_gate = pltpu.with_memory_space_constraint(w_gate, pltpu.HBM)
        w_up = pltpu.with_memory_space_constraint(w_up, pltpu.HBM)
    return pl.pallas_call(
        load_gate_up_kernel if load else gate_up_kernel,
        out_shape=[out] * blocks + held,
        in_specs=[pl.BlockSpec(memory_space=pltpu.SMEM)] + [VM] * 2 + [ANY if load else VM] * 2,
        out_specs=[VM] * (blocks + len(held)),
        scratch_shapes=scratch,
        compiler_params=pltpu.CompilerParams(vmem_limit_bytes=12 * 1024 * 1024),
        cost_estimate=pl.CostEstimate(
            flops=4 * rows * width * hidden, transcendentals=0, bytes_accessed=4 * width * hidden + 4 * rows * hidden
        ),
    )(order, x, gain, w_gate, w_up)


def small_call(kernel, outs, *arrays, after=(), weight=0):
    def body(*refs):
        kernel(*refs[: len(arrays)], *refs[len(arrays) + len(after) :])

    return pl.pallas_call(
        body,
        out_shape=[jax.ShapeDtypeStruct(shape, dtype) for shape, dtype in outs],
        in_specs=[VM] * len(arrays) + [ANY] * len(after),
        out_specs=[VM] * len(outs),
        compiler_params=pltpu.CompilerParams(vmem_limit_bytes=8 * 1024 * 1024),
        cost_estimate=pl.CostEstimate(flops=weight, transcendentals=0, bytes_accessed=0) if weight else None,
    )(*arrays, *after)


def line_sum_kernel(a0, a1, a2, a3, keep, go):
    unit, wide = keep.shape
    for start in range(0, wide, 128):
        at = slice(start, start + 128)
        for lo, out in ((0, keep), (unit, go)):
            rows = slice(lo, lo + unit)
            total = f32(a0[rows, at]) + f32(a1[rows, at]) + f32(a2[rows, at]) + f32(a3[rows, at])
            out[:, at] = total.astype(out.dtype)


def pair_sum_kernel(b0, b1, *outs):
    unit, wide = outs[0].shape
    for start in range(0, wide, 128):
        at = slice(start, start + 128)
        for n, out in enumerate(outs):
            rows = slice(n * unit, (n + 1) * unit)
            out[:, at] = (f32(b0[rows, at]) + f32(b1[rows, at])).astype(out.dtype)


def activate_kernel(keep, *refs):
    others, out = refs[:-1], refs[-1]
    hidden = out.shape[1]

    def summed(start):
        at = slice(start, start + 128)
        value = keep[:, at]
        for other in others:
            value = value + f32(other[:, at])
        return value

    squares = jnp.sum(summed(2 * hidden), axis=1, keepdims=True)
    scale = lax.rsqrt(squares / D + 1e-05) * UP
    for start in range(0, hidden, 128):
        gate = summed(start) * scale
        up = summed(hidden + start) * scale
        out[:, start : start + 128] = (gate / (1.0 + jnp.exp(-gate)) * up).astype(jnp.bfloat16)


def stack_kernel(*refs):
    parts, out = refs[:-1], refs[-1]
    unit = parts[0].shape[0]
    for n, part in enumerate(parts):
        out[n * unit : (n + 1) * unit, :] = part[...]


def down_kernel(count, order_a, order_b, *refs):
    pieces, w_ref, out_a, out_b, hidden = refs[:-4], *refs[-4:]
    half = hidden.shape[0] // 2
    unit = half // 8
    for base, order, group in ((0, order_a, pieces[:count]), (half, order_b, pieces[count:])):
        per = group[0].shape[0] // unit
        for n in range(8):
            start = pl.multiple_of(order[n] * unit, unit)
            at = (n % per) * unit
            hidden[pl.ds(base + start, unit), :] = group[n // per][at : at + unit, :]
    for start in range(0, w_ref.shape[1], 256):
        result = jnp.dot(hidden[...], w_ref[:, start : start + 256], preferred_element_type=jnp.float32)
        result = result.astype(jnp.bfloat16)
        out_a[:, start : start + 256] = result[:half]
        out_b[:, start : start + 256] = result[half:]


def down(order_a, order_b, pieces_a, pieces_b, w_down):
    rows = sum(piece.shape[0] for piece in pieces_a)
    inner, width = w_down.shape
    pieces = [*pieces_a, *pieces_b]
    return pl.pallas_call(
        functools.partial(down_kernel, len(pieces_a)),
        out_shape=[jax.ShapeDtypeStruct((rows, width), jnp.bfloat16)] * 2,
        in_specs=[pl.BlockSpec(memory_space=pltpu.SMEM)] * 2 + [VM] * (len(pieces) + 1),
        out_specs=[VM] * 2,
        scratch_shapes=[pltpu.VMEM((2 * rows, inner), jnp.bfloat16)],
        compiler_params=pltpu.CompilerParams(vmem_limit_bytes=10 * 1024 * 1024),
    )(order_a, order_b, *pieces, w_down)


def qkv_kernel(mine_ref, other_ref, src_ref, dst_ref, w_ref, *refs):
    outs, ordered = refs[:-1], refs[-1]
    half = mine_ref.shape[0]
    pick = jnp.where(dst_ref[...] == src_ref[...], 1.0, 0.0).astype(jnp.bfloat16)
    for start in range(0, mine_ref.shape[1], 512):
        at = slice(start, start + 512)
        rows = jnp.dot(pick[:, :half], mine_ref[:, at], preferred_element_type=jnp.float32)
        rows = rows + jnp.dot(pick[:, half:], other_ref[:, at], preferred_element_type=jnp.float32)
        ordered[:, at] = rows.astype(jnp.bfloat16)
    wide = w_ref.shape[2]
    for part in range(w_ref.shape[0]):
        result = jnp.dot(ordered[...], w_ref[part], preferred_element_type=jnp.float32).astype(jnp.bfloat16)
        spread(outs, result, part * wide)


def slot_qkv(mine, other, key_src, key_dst, w_parts):
    half, width = mine.shape
    rows = 2 * half
    parts, _, wide = w_parts.shape
    return pl.pallas_call(
        qkv_kernel,
        out_shape=[jax.ShapeDtypeStruct((rows // 8, parts * wide), jnp.bfloat16)] * 8,
        in_specs=[VM] * 5,
        out_specs=[VM] * 8,
        scratch_shapes=[pltpu.VMEM((rows, width), jnp.bfloat16)],
        compiler_params=pltpu.CompilerParams(vmem_limit_bytes=12 * 1024 * 1024),
        cost_estimate=pl.CostEstimate(
            flops=2 * rows * width * (parts * wide + rows),
            transcendentals=0,
            bytes_accessed=2 * width * (parts * wide + rows),
        ),
    )(mine, other, key_src, key_dst, w_parts)


def per_device(
    states,
    norm_gain,
    w_gate,
    w_up,
    w_down,
    w_qkv,
    w_class,
    cache_keys,
    cache_values,
    cache_lengths,
    row_slots,
):
    steps = states.shape[0]
    local_rows = states.shape[1]
    width = states.shape[2]
    hidden_here = w_gate.shape[1]
    owner_rows = cache_keys.shape[0]
    history = cache_keys.shape[1]
    local_width = w_qkv.shape[2]
    heads_here = local_width // HEAD_DIM
    total_rows = row_slots.shape[0]
    rows = steps * total_rows
    per = steps * local_rows
    block = rows // 8
    unit = block // 2
    tx = lax.axis_index("tx")
    ty = lax.axis_index("ty")
    my_y, my_zh = tx % 4, tx // 4

    def to(dy, dz):
        return (my_zh ^ dz) * 4 + (my_y + dy) % 4

    def source(dy, dz):
        return (my_zh ^ dz) * 4 + (my_y - dy + 4) % 4

    y_major = [(dy, dz) for dy in range(4) for dz in range(2)]
    z_major = [(dy, dz) for dz in range(2) for dy in range(4)]
    send_a = jnp.stack([to(*m) for m in y_major])
    send_b = jnp.stack([to(*m) for m in z_major])
    from_a = jnp.stack([source(*m) for m in y_major])
    from_b = jnp.stack([source(*m) for m in z_major])

    pos = jnp.arange(rows, dtype=jnp.int32)
    chunk = pos // per
    source_ty = 2 * (chunk % 8) + ((ty % 2) ^ (chunk // 8))
    row_of = source_ty * local_rows + pos % local_rows
    hit = row_of[:, None] == jnp.arange(total_rows, dtype=jnp.int32)[None, :]
    slot_of = jnp.sum(jnp.where(hit, row_slots[None, :], 0), axis=1)
    key_src = (((pos % per) // local_rows) * total_rows + slot_of)[None, :]
    moves = [(0, 0), (2, 1), (1, 1), (3, 1), (2, 0), (0, 1), (1, 0), (3, 0)]
    target = jnp.zeros((rows,), jnp.int32)
    for n, move in enumerate(moves):
        target = jnp.where(pos // block == n, to(*move), target)
    key_dst = ((pos % block) // owner_rows) * total_rows + target * owner_rows + pos % owner_rows
    key_dst = key_dst[:, None]

    own = states.reshape(per, width)
    gain = norm_gain[None, :]
    mine, other = gather_ty(own)
    *part_a, w_gate, w_up = gate_up(send_a, mine, gain, w_gate, w_up, 4, True)
    part_b = gate_up(send_b, other, gain, w_gate, w_up, 2, False)
    half_send = (unit, part_a[0].shape[1])
    came_a = [tx_move(part_a[dy], dy, 0) for dy in (2, 1, 3)]
    came_b = tx_move(part_b[1], 0, 1)
    keep = (half_send, jnp.float32)
    go = (half_send, jnp.bfloat16)
    keep_a, go_a = small_call(line_sum_kernel, [keep, go], part_a[0], *came_a, weight=5000000000)
    keep_b, *go_b = small_call(pair_sum_kernel, [keep, go, go, go], part_b[0], came_b, after=(go_a,))
    came_b = [tx_move(go_b[dy - 1], dy, 0) for dy in (2, 1, 3)]
    came_a = tx_move(go_a, 0, 1)
    half_hidden = ((unit, hidden_here), jnp.bfloat16)
    (hidden_a,) = small_call(activate_kernel, [half_hidden], keep_a, came_a)
    came_a = tx_move(hidden_a, 0, 1)
    (pair_a,) = small_call(stack_kernel, [((2 * unit, hidden_here), jnp.bfloat16)], hidden_a, came_a)
    (hidden_b,) = small_call(activate_kernel, [half_hidden], keep_b, *came_b, after=(pair_a,))
    came_b = [tx_move(hidden_b, dy, 0) for dy in (2, 1, 3)]
    (line_b,) = small_call(stack_kernel, [((4 * unit, hidden_here), jnp.bfloat16)], hidden_b, came_b[1], came_b[0], came_b[2])
    pieces_a = [pair_a] + [tx_move(pair_a, dy, 0) for dy in (1, 2, 3)]
    pieces_b = [line_b, tx_move(line_b, 0, 1)]
    w_down = fetch(w_down, 4, pair_a)
    mixed_a, mixed_b = down(from_a, from_b, pieces_a, pieces_b, w_down)
    chip = (f32(mixed_a) + f32(core_swap(mixed_b))).astype(jnp.bfloat16)
    parts = chip_exchange(chip.reshape(8, per, width))
    stream = (f32(own) + jnp.sum(f32(parts), axis=0)).astype(jnp.bfloat16)
    stream_out = stream.reshape(steps, local_rows, width)

    mine, other = gather_ty(stream)
    w_parts = fetch(jnp.transpose(w_qkv, (1, 0, 2)), 3, mine)
    qkv = slot_qkv(mine, other, key_src, key_dst, w_parts)
    triple = f32(qkv[0])
    for piece, move in zip(qkv[1:], moves[1:]):
        triple = triple + f32(tx_move(piece, *move))
    triple = triple.astype(jnp.bfloat16)
    triple = triple.reshape(steps, owner_rows, 3, heads_here, HEAD_DIM)
    query, new_keys, new_vals = triple[:, :, 0], triple[:, :, 1], triple[:, :, 2]
    keys_h = cache_keys.reshape(owner_rows, history, heads_here, HEAD_DIM)
    vals_h = cache_values.reshape(owner_rows, history, heads_here, HEAD_DIM)
    old = jnp.einsum("tshd,slhd->tshl", query, keys_h, preferred_element_type=jnp.float32)
    new = jnp.einsum("tshd,ushd->tshu", query, new_keys, preferred_element_type=jnp.float32)
    old = old * HEAD_DIM ** (-0.5)
    new = new * HEAD_DIM ** (-0.5)
    where_pos = jnp.arange(history, dtype=jnp.int32)
    old = jnp.where((where_pos[None, :] < cache_lengths[:, None])[None, :, None, :], old, jnp.float32(-1e30))
    causal = jnp.arange(steps)[:, None] >= jnp.arange(steps)[None, :]
    new = jnp.where(causal[:, None, None, :], new, jnp.float32(-1e30))
    top = jnp.maximum(jnp.max(old, axis=3, keepdims=True), jnp.max(new, axis=3, keepdims=True))
    old = jnp.exp(old - top)
    new = jnp.exp(new - top)
    denom = jnp.sum(old, axis=3, keepdims=True) + jnp.sum(new, axis=3, keepdims=True)
    old = (old / denom).astype(jnp.bfloat16)
    new = (new / denom).astype(jnp.bfloat16)
    attended = jnp.einsum("tshl,slhd->tshd", old, vals_h, preferred_element_type=jnp.float32)
    attended = attended + jnp.einsum("tshu,ushd->tshd", new, new_vals, preferred_element_type=jnp.float32)
    attended = attended.reshape(steps * owner_rows, local_width).astype(jnp.bfloat16)
    part = jnp.einsum("rf,fk->kr", attended, w_class, preferred_element_type=jnp.float32)
    classes = part.shape[0]
    packed = jnp.concatenate([part[: classes // 2], part[classes // 2 :]], axis=1)
    packed = jnp.pad(packed, ((0, 1), (0, 0)))
    spread = lax.all_to_all(jnp.broadcast_to(packed[None], (128,) + packed.shape), ("tx", "ty"), 0, 0)
    by_tx = jnp.sum(spread.reshape(8, 16, 8, 128), axis=1)[:, : classes // 2]
    by_tx = by_tx.reshape(8, classes // 2, 2, steps, owner_rows)
    by_slot = by_tx.transpose(2, 1, 3, 0, 4).reshape(classes * steps, total_rows)
    pick = (jnp.arange(total_rows)[:, None] == row_slots[None, :]).astype(jnp.float32)
    logits = jnp.dot(by_slot, pick, precision=lax.Precision.HIGHEST, preferred_element_type=jnp.float32)
    category_logits = logits.reshape(classes, steps, total_rows).transpose(1, 2, 0)
    return (stream_out, category_logits)


def solution(mesh):
    return jax.shard_map(
        per_device,
        mesh=mesh,
        in_specs=(
            P(None, "ty", "tx"),
            P("tx"),
            P("tx", "ty"),
            P("tx", "ty"),
            P("ty", "tx"),
            P("tx", None, "ty"),
            P("ty", None),
            P("tx", None, "ty"),
            P("tx", None, "ty"),
            P("tx"),
            P(),
        ),
        out_specs=(P(None, "ty", "tx"), P()),
        check_vma=False,
    )
```

```python
import functools

import jax
import jax.numpy as jnp
from jax import lax
from jax.experimental import pallas as pl
from jax.experimental.pallas import tpu as pltpu
from jax.sharding import PartitionSpec as P

D = 16384
HEAD_DIM = 128
DOWN = 2.0 ** -24
UP = 2.0 ** 24


def tx_move(array, dy, dz):
    pairs = [(z * 4 + y, (z ^ dz) * 4 + (y + dy) % 4) for z in range(2) for y in range(4)]
    return lax.ppermute(array, "tx", pairs)


def core_swap(array):
    return lax.ppermute(array, "ty", [(n, n ^ 1) for n in range(16)])


def chip_exchange(blocks):
    groups = [[2 * n + c for n in range(8)] for c in range(2)]
    return lax.all_to_all(blocks, "ty", 0, 0, axis_index_groups=groups)


def gather_ty(rows):
    mine = chip_exchange(jnp.broadcast_to(rows[None], (8,) + rows.shape))
    mine = mine.reshape(8 * rows.shape[0], rows.shape[1])
    return mine, core_swap(mine)


def f32(array):
    return array.astype(jnp.float32)


VM = pl.BlockSpec(memory_space=pltpu.VMEM)
ANY = pl.BlockSpec(memory_space=pl.ANY)
SMEM = pl.BlockSpec(memory_space=pltpu.SMEM)


def fetch_kernel(source, *refs):
    target, sems = refs[-2:]
    copies = []
    part = source.shape[0] // sems.shape[0]
    for n in range(sems.shape[0]):
        at = pl.ds(n * part, part)
        copies.append(pltpu.make_async_copy(source.at[at], target.at[at], sems.at[n]))
    for copy in copies:
        copy.start()
    for copy in copies:
        copy.wait()


def fetch(array, pieces, *after):
    return pl.pallas_call(
        fetch_kernel,
        out_shape=pltpu.VMEM(array.shape, array.dtype),
        in_specs=[ANY] * (1 + len(after)),
        out_specs=VM,
        scratch_shapes=[pltpu.SemaphoreType.DMA((pieces,))],
        compiler_params=pltpu.CompilerParams(vmem_limit_bytes=2 * 1024 * 1024),
    )(pltpu.with_memory_space_constraint(array, pltpu.HBM), *after)


def scale_rows(order, x_ref, gain_ref, hidden, outs, scaled):
    rows = outs[0].shape[0]
    unit = x_ref.shape[0] // 8
    gain = gain_ref[...].astype(jnp.float32) * DOWN
    lane = lax.broadcasted_iota(jnp.int32, (unit, 128), 1)
    for n in range(8):
        start = pl.multiple_of(order[n] * unit, unit)
        values = x_ref[pl.ds(start, unit), :].astype(jnp.float32)
        scaled[n * unit : (n + 1) * unit, :] = (values * gain).astype(jnp.bfloat16)
        squares = jnp.sum(values * values, axis=1, keepdims=True)
        first = squares.astype(jnp.bfloat16).astype(jnp.float32)
        second = (squares - first).astype(jnp.bfloat16).astype(jnp.float32)
        third = squares - first - second
        columns = jnp.where(lane == 0, first, jnp.where(lane == 1, second, jnp.where(lane == 2, third, 0.0)))
        at = (n * unit) % rows
        outs[n * unit // rows][at : at + unit, 2 * hidden :] = columns.astype(jnp.bfloat16)


def spread(outs, result, start):
    rows = outs[0].shape[0]
    for n, out in enumerate(outs):
        out[:, start : start + result.shape[1]] = result[n * rows : (n + 1) * rows]


def load_gate_up_kernel(order, x_ref, gain_ref, wg_hbm, wu_hbm, *refs):
    outs, scaled, half_sum, wg_ref, wu_ref, sems = refs[:-5], *refs[-5:]
    width, hidden = wg_ref.shape
    half, part = width // 2, width // 4
    groups = []
    for n, (source, target) in enumerate(((wg_hbm, wg_ref), (wu_hbm, wu_ref))):
        for m in range(2):
            rows = [pl.ds(m * half + k * part, part) for k in range(2)]
            groups.append(
                [
                    pltpu.make_async_copy(source.at[row], target.at[row], sems.at[4 * n + 2 * m + k])
                    for k, row in enumerate(rows)
                ]
            )
    for copy in groups[0] + groups[1]:
        copy.start()
    scale_rows(order, x_ref, gain_ref, hidden, outs, scaled)
    for n, w_ref in enumerate((wg_ref, wu_ref)):
        for m in range(2):
            for copy in groups[2 * n + m]:
                copy.wait()
            if n == 0:
                for copy in groups[2 + m]:
                    copy.start()
            k = slice(m * half, (m + 1) * half)
            for start in range(0, hidden, 256):
                at = slice(start, min(start + 256, hidden))
                result = jnp.dot(scaled[:, k], w_ref[k, at], preferred_element_type=jnp.float32)
                if m == 0:
                    half_sum[:, at] = result
                else:
                    spread(outs, (half_sum[:, at] + result).astype(jnp.bfloat16), n * hidden + start)


def gate_up(order, x, gain, w_gate, w_up, blocks):
    rows, width = x.shape
    hidden = w_gate.shape[1]
    space = pltpu.HBM if blocks == 2 else pltpu.VMEM
    out = space((rows // blocks, 2 * hidden + 128), jnp.bfloat16)
    w_gate = pltpu.with_memory_space_constraint(w_gate, pltpu.HBM)
    w_up = pltpu.with_memory_space_constraint(w_up, pltpu.HBM)
    return pl.pallas_call(
        load_gate_up_kernel,
        out_shape=[out] * blocks,
        in_specs=[SMEM] + [VM] * 2 + [ANY] * 2,
        out_specs=[VM] * blocks,
        scratch_shapes=[
            pltpu.VMEM((rows, width), jnp.bfloat16),
            pltpu.VMEM((rows, hidden), jnp.float32),
            pltpu.VMEM(w_gate.shape, w_gate.dtype),
            pltpu.VMEM(w_up.shape, w_up.dtype),
            pltpu.SemaphoreType.DMA((8,)),
        ],
        compiler_params=pltpu.CompilerParams(vmem_limit_bytes=24 * 1024 * 1024),
        cost_estimate=pl.CostEstimate(
            flops=4 * rows * width * hidden, transcendentals=0, bytes_accessed=4 * width * hidden + 4 * rows * hidden
        ),
    )(order, x, gain, w_gate, w_up)


def small_call(kernel, outs, *arrays, after=(), weight=0):
    def body(*refs):
        kernel(*refs[: len(arrays)], *refs[len(arrays) + len(after) :])

    return pl.pallas_call(
        body,
        out_shape=[jax.ShapeDtypeStruct(shape, dtype) for shape, dtype in outs],
        in_specs=[VM] * len(arrays) + [ANY] * len(after),
        out_specs=[VM] * len(outs),
        compiler_params=pltpu.CompilerParams(vmem_limit_bytes=8 * 1024 * 1024),
        cost_estimate=pl.CostEstimate(flops=weight, transcendentals=0, bytes_accessed=0) if weight else None,
    )(*arrays, *after)


def line_sum_kernel(a0, a1, a2, a3, keep, go):
    unit, wide = keep.shape
    for start in range(0, wide, 128):
        at = slice(start, start + 128)
        for lo, out in ((0, keep), (unit, go)):
            rows = slice(lo, lo + unit)
            total = f32(a0[rows, at]) + f32(a1[rows, at]) + f32(a2[rows, at]) + f32(a3[rows, at])
            out[:, at] = total.astype(out.dtype)


def pair_sum_kernel(b0, b1, *outs):
    unit, wide = outs[0].shape
    for start in range(0, wide, 128):
        at = slice(start, start + 128)
        for n, out in enumerate(outs):
            rows = slice(n * unit, (n + 1) * unit)
            out[:, at] = (f32(b0[rows, at]) + f32(b1[rows, at])).astype(out.dtype)


def activate_kernel(keep, *refs):
    others, out = refs[:-1], refs[-1]
    hidden = out.shape[1]

    def summed(start):
        at = slice(start, start + 128)
        value = keep[:, at]
        for other in others:
            value = value + f32(other[:, at])
        return value

    squares = jnp.sum(summed(2 * hidden), axis=1, keepdims=True)
    scale = lax.rsqrt(squares / D + 1e-05) * UP
    for start in range(0, hidden, 128):
        gate = summed(start) * scale
        up = summed(hidden + start) * scale
        out[:, start : start + 128] = (gate / (1.0 + jnp.exp(-gate)) * up).astype(jnp.bfloat16)


def stack_kernel(*refs):
    parts, out = refs[:-1], refs[-1]
    unit = parts[0].shape[0]
    for n, part in enumerate(parts):
        out[n * unit : (n + 1) * unit, :] = part[...]


def put_blocks(order, pieces, target, base, unit):
    per = pieces[0].shape[0] // unit
    for n in range(8):
        start = pl.multiple_of(order[n] * unit, unit)
        at = (n % per) * unit
        target[pl.ds(base + start, unit), :] = pieces[n // per][at : at + unit, :]


def place_kernel(order, *refs):
    put_blocks(order, refs[:-1], refs[-1], 0, refs[-1].shape[0] // 8)


def place(order, pieces, weight):
    rows = sum(piece.shape[0] for piece in pieces)
    return pl.pallas_call(
        place_kernel,
        out_shape=jax.ShapeDtypeStruct((rows, pieces[0].shape[1]), pieces[0].dtype),
        in_specs=[SMEM] + [VM] * len(pieces),
        out_specs=VM,
        compiler_params=pltpu.CompilerParams(vmem_limit_bytes=4 * 1024 * 1024),
        cost_estimate=pl.CostEstimate(flops=weight, transcendentals=0, bytes_accessed=0),
    )(order, *pieces)


def down_kernel(order_b, placed, *refs):
    pieces, w_ref, out_a, out_b, hidden = refs[:-4], *refs[-4:]
    half = hidden.shape[0] // 2
    hidden[:half, :] = placed[...]
    put_blocks(order_b, pieces, hidden, half, half // 8)
    for start in range(0, w_ref.shape[1], 256):
        result = jnp.dot(hidden[...], w_ref[:, start : start + 256], preferred_element_type=jnp.float32)
        result = result.astype(jnp.bfloat16)
        out_a[:, start : start + 256] = result[:half]
        out_b[:, start : start + 256] = result[half:]


def down(order_b, placed, pieces_b, w_down):
    rows = placed.shape[0]
    inner, width = w_down.shape
    return pl.pallas_call(
        down_kernel,
        out_shape=[jax.ShapeDtypeStruct((rows, width), jnp.bfloat16)] * 2,
        in_specs=[SMEM] + [VM] * (len(pieces_b) + 2),
        out_specs=[VM] * 2,
        scratch_shapes=[pltpu.VMEM((2 * rows, inner), jnp.bfloat16)],
        compiler_params=pltpu.CompilerParams(vmem_limit_bytes=10 * 1024 * 1024),
    )(order_b, placed, *pieces_b, w_down)


def qkv_kernel(mine_ref, other_ref, src_ref, dst_ref, w_ref, *refs):
    outs, ordered = refs[:-1], refs[-1]
    half = mine_ref.shape[0]
    pick = jnp.where(dst_ref[...] == src_ref[...], 1.0, 0.0).astype(jnp.bfloat16)
    for start in range(0, mine_ref.shape[1], 512):
        at = slice(start, start + 512)
        rows = jnp.dot(pick[:, :half], mine_ref[:, at], preferred_element_type=jnp.float32)
        rows = rows + jnp.dot(pick[:, half:], other_ref[:, at], preferred_element_type=jnp.float32)
        ordered[:, at] = rows.astype(jnp.bfloat16)
    wide = w_ref.shape[2]
    for part in range(w_ref.shape[0]):
        result = jnp.dot(ordered[...], w_ref[part], preferred_element_type=jnp.float32).astype(jnp.bfloat16)
        spread(outs, result, part * wide)


def slot_qkv(mine, other, key_src, key_dst, w_parts):
    half, width = mine.shape
    rows = 2 * half
    parts, _, wide = w_parts.shape
    return pl.pallas_call(
        qkv_kernel,
        out_shape=[jax.ShapeDtypeStruct((rows // 8, parts * wide), jnp.bfloat16)] * 8,
        in_specs=[VM] * 5,
        out_specs=[VM] * 8,
        scratch_shapes=[pltpu.VMEM((rows, width), jnp.bfloat16)],
        compiler_params=pltpu.CompilerParams(vmem_limit_bytes=12 * 1024 * 1024),
        cost_estimate=pl.CostEstimate(
            flops=2 * rows * width * (parts * wide + rows),
            transcendentals=0,
            bytes_accessed=2 * width * (parts * wide + rows),
        ),
    )(mine, other, key_src, key_dst, w_parts)


def per_device(
    states,
    norm_gain,
    w_gate,
    w_up,
    w_down,
    w_qkv,
    w_class,
    cache_keys,
    cache_values,
    cache_lengths,
    row_slots,
):
    steps = states.shape[0]
    local_rows = states.shape[1]
    width = states.shape[2]
    hidden_here = w_gate.shape[1]
    owner_rows = cache_keys.shape[0]
    history = cache_keys.shape[1]
    local_width = w_qkv.shape[2]
    heads_here = local_width // HEAD_DIM
    total_rows = row_slots.shape[0]
    rows = steps * total_rows
    per = steps * local_rows
    block = rows // 8
    unit = block // 2
    tx = lax.axis_index("tx")
    ty = lax.axis_index("ty")
    my_y, my_zh = tx % 4, tx // 4

    def to(dy, dz):
        return (my_zh ^ dz) * 4 + (my_y + dy) % 4

    def source(dy, dz):
        return (my_zh ^ dz) * 4 + (my_y - dy + 4) % 4

    y_major = [(dy, dz) for dy in range(4) for dz in range(2)]
    z_major = [(dy, dz) for dz in range(2) for dy in range(4)]
    send_a = jnp.stack([to(*m) for m in y_major])
    send_b = jnp.stack([to(*m) for m in z_major])
    from_a = jnp.stack([source(*m) for m in y_major])
    from_b = jnp.stack([source(*m) for m in z_major])

    pos = jnp.arange(rows, dtype=jnp.int32)
    chunk = pos // per
    source_ty = 2 * (chunk % 8) + ((ty % 2) ^ (chunk // 8))
    row_of = source_ty * local_rows + pos % local_rows
    hit = row_of[:, None] == jnp.arange(total_rows, dtype=jnp.int32)[None, :]
    slot_of = jnp.sum(jnp.where(hit, row_slots[None, :], 0), axis=1)
    key_src = (((pos % per) // local_rows) * total_rows + slot_of)[None, :]
    moves = [(0, 0), (2, 1), (1, 1), (3, 1), (2, 0), (0, 1), (1, 0), (3, 0)]
    target = jnp.zeros((rows,), jnp.int32)
    for n, move in enumerate(moves):
        target = jnp.where(pos // block == n, to(*move), target)
    key_dst = ((pos % block) // owner_rows) * total_rows + target * owner_rows + pos % owner_rows
    key_dst = key_dst[:, None]

    own = states.reshape(per, width)
    gain = norm_gain[None, :]
    mine, other = gather_ty(own)
    part_b = gate_up(send_b, mine, gain, w_gate, w_up, 2)
    part_a = gate_up(send_a, other, gain, w_gate, w_up, 4)
    half_send = (unit, part_a[0].shape[1])
    keep = (half_send, jnp.float32)
    go = (half_send, jnp.bfloat16)
    half_hidden = ((unit, hidden_here), jnp.bfloat16)
    came_b = tx_move(part_b[1], 0, 1)
    came_a = [tx_move(part_a[dy], dy, 0) for dy in (2, 1, 3)]
    keep_b, *go_b = small_call(pair_sum_kernel, [keep, go, go, go], part_b[0], came_b)
    came_b = [tx_move(go_b[dy - 1], dy, 0) for dy in (2, 1, 3)]
    keep_a, go_a = small_call(line_sum_kernel, [keep, go], part_a[0], *came_a, after=(go_b[0],))
    came_a = tx_move(go_a, 0, 1)
    (hidden_b,) = small_call(activate_kernel, [half_hidden], keep_b, *came_b, after=(go_a,))
    came_b = [tx_move(hidden_b, dy, 0) for dy in (2, 1, 3)]
    (hidden_a,) = small_call(activate_kernel, [half_hidden], keep_a, came_a, after=(hidden_b,))
    came_a = tx_move(hidden_a, 0, 1)
    (pair_a,) = small_call(stack_kernel, [((2 * unit, hidden_here), jnp.bfloat16)], hidden_a, came_a)
    (line_b,) = small_call(
        stack_kernel, [((4 * unit, hidden_here), jnp.bfloat16)], hidden_b, came_b[1], came_b[0], came_b[2], after=(pair_a,)
    )
    pieces_a = [pair_a] + [tx_move(pair_a, dy, 0) for dy in (1, 2, 3)]
    pieces_b = [line_b, tx_move(line_b, 0, 1)]
    w_down = fetch(w_down, 4, pair_a)
    placed = place(from_a, pieces_a, 2500000000)
    mixed_a, mixed_b = down(from_b, placed, pieces_b, w_down)
    chip = (f32(mixed_b) + f32(core_swap(mixed_a))).astype(jnp.bfloat16)
    parts = chip_exchange(chip.reshape(8, per, width))
    stream = (f32(own) + jnp.sum(f32(parts), axis=0)).astype(jnp.bfloat16)
    stream_out = stream.reshape(steps, local_rows, width)

    mine, other = gather_ty(stream)
    w_parts = fetch(jnp.transpose(w_qkv, (1, 0, 2)), 3, mine)
    qkv = slot_qkv(mine, other, key_src, key_dst, w_parts)
    triple = f32(qkv[0])
    for piece, move in zip(qkv[1:], moves[1:]):
        triple = triple + f32(tx_move(piece, *move))
    triple = triple.astype(jnp.bfloat16)
    triple = triple.reshape(steps, owner_rows, 3, heads_here, HEAD_DIM)
    query, new_keys, new_vals = triple[:, :, 0], triple[:, :, 1], triple[:, :, 2]
    keys_h = cache_keys.reshape(owner_rows, history, heads_here, HEAD_DIM)
    vals_h = cache_values.reshape(owner_rows, history, heads_here, HEAD_DIM)
    old = jnp.einsum("tshd,slhd->tshl", query, keys_h, preferred_element_type=jnp.float32)
    new = jnp.einsum("tshd,ushd->tshu", query, new_keys, preferred_element_type=jnp.float32)
    old = old * HEAD_DIM ** (-0.5)
    new = new * HEAD_DIM ** (-0.5)
    where_pos = jnp.arange(history, dtype=jnp.int32)
    old = jnp.where((where_pos[None, :] < cache_lengths[:, None])[None, :, None, :], old, jnp.float32(-1e30))
    causal = jnp.arange(steps)[:, None] >= jnp.arange(steps)[None, :]
    new = jnp.where(causal[:, None, None, :], new, jnp.float32(-1e30))
    top = jnp.maximum(jnp.max(old, axis=3, keepdims=True), jnp.max(new, axis=3, keepdims=True))
    old = jnp.exp(old - top)
    new = jnp.exp(new - top)
    denom = jnp.sum(old, axis=3, keepdims=True) + jnp.sum(new, axis=3, keepdims=True)
    old = (old / denom).astype(jnp.bfloat16)
    new = (new / denom).astype(jnp.bfloat16)
    attended = jnp.einsum("tshl,slhd->tshd", old, vals_h, preferred_element_type=jnp.float32)
    attended = attended + jnp.einsum("tshu,ushd->tshd", new, new_vals, preferred_element_type=jnp.float32)
    attended = attended.reshape(steps * owner_rows, local_width).astype(jnp.bfloat16)
    part = jnp.einsum("rf,fk->kr", attended, w_class, preferred_element_type=jnp.float32)
    classes = part.shape[0]
    packed = jnp.concatenate([part[: classes // 2], part[classes // 2 :]], axis=1)
    packed = jnp.pad(packed, ((0, 1), (0, 0)))
    spread = lax.all_to_all(jnp.broadcast_to(packed[None], (128,) + packed.shape), ("tx", "ty"), 0, 0)
    by_tx = jnp.sum(spread.reshape(8, 16, 8, 128), axis=1)[:, : classes // 2]
    by_tx = by_tx.reshape(8, classes // 2, 2, steps, owner_rows)
    by_slot = by_tx.transpose(2, 1, 3, 0, 4).reshape(classes * steps, total_rows)
    pick = (jnp.arange(total_rows)[:, None] == row_slots[None, :]).astype(jnp.float32)
    logits = jnp.dot(by_slot, pick, precision=lax.Precision.HIGHEST, preferred_element_type=jnp.float32)
    category_logits = logits.reshape(classes, steps, total_rows).transpose(1, 2, 0)
    return (stream_out, category_logits)


def solution(mesh):
    return jax.shard_map(
        per_device,
        mesh=mesh,
        in_specs=(
            P(None, "ty", "tx"),
            P("tx"),
            P("tx", "ty"),
            P("tx", "ty"),
            P("ty", "tx"),
            P("tx", None, "ty"),
            P("ty", None),
            P("tx", None, "ty"),
            P("tx", None, "ty"),
            P("tx"),
            P(),
        ),
        out_specs=(P(None, "ty", "tx"), P()),
        check_vma=False,
    )
```

```python
import functools

import jax
import jax.numpy as jnp
from jax import lax
from jax.experimental import pallas as pl
from jax.experimental.pallas import tpu as pltpu
from jax.sharding import PartitionSpec as P

D = 16384
HEAD_DIM = 128
DOWN = 2.0 ** -24
UP = 2.0 ** 24


def tx_move(array, dy, dz):
    pairs = [(z * 4 + y, (z ^ dz) * 4 + (y + dy) % 4) for z in range(2) for y in range(4)]
    return lax.ppermute(array, "tx", pairs)


def core_swap(array):
    return lax.ppermute(array, "ty", [(n, n ^ 1) for n in range(16)])


def chip_exchange(blocks):
    groups = [[2 * n + c for n in range(8)] for c in range(2)]
    return lax.all_to_all(blocks, "ty", 0, 0, axis_index_groups=groups)


def gather_ty(rows):
    mine = chip_exchange(jnp.broadcast_to(rows[None], (8,) + rows.shape))
    mine = mine.reshape(8 * rows.shape[0], rows.shape[1])
    return mine, core_swap(mine)


def f32(array):
    return array.astype(jnp.float32)


VM = pl.BlockSpec(memory_space=pltpu.VMEM)
ANY = pl.BlockSpec(memory_space=pl.ANY)
SMEM = pl.BlockSpec(memory_space=pltpu.SMEM)


def fetch_kernel(source, *refs):
    target, sems = refs[-2:]
    copies = []
    part = source.shape[0] // sems.shape[0]
    for n in range(sems.shape[0]):
        at = pl.ds(n * part, part)
        copies.append(pltpu.make_async_copy(source.at[at], target.at[at], sems.at[n]))
    for copy in copies:
        copy.start()
    for copy in copies:
        copy.wait()


def fetch(array, pieces, *after):
    return pl.pallas_call(
        fetch_kernel,
        out_shape=pltpu.VMEM(array.shape, array.dtype),
        in_specs=[ANY] * (1 + len(after)),
        out_specs=VM,
        scratch_shapes=[pltpu.SemaphoreType.DMA((pieces,))],
        compiler_params=pltpu.CompilerParams(vmem_limit_bytes=2 * 1024 * 1024),
    )(pltpu.with_memory_space_constraint(array, pltpu.HBM), *after)


def blocks_of(outs):
    found, at = [], 0
    for out in outs:
        found.append((out, at, out.shape[0]))
        at += out.shape[0]
    return found


def scale_rows(orders, x_ref, gain_ref, hidden, outs, scaled):
    unit = x_ref.shape[0] // 16
    gain = gain_ref[...].astype(jnp.float32) * DOWN
    lane = lax.broadcasted_iota(jnp.int32, (unit, 128), 1)
    for n in range(16):
        start = pl.multiple_of(orders[n // 8][n % 8] * (2 * unit) + (n // 8) * unit, unit)
        values = x_ref[pl.ds(start, unit), :].astype(jnp.float32)
        to = n * unit
        scaled[to : to + unit, :] = (values * gain).astype(jnp.bfloat16)
        squares = jnp.sum(values * values, axis=1, keepdims=True)
        first = squares.astype(jnp.bfloat16).astype(jnp.float32)
        second = (squares - first).astype(jnp.bfloat16).astype(jnp.float32)
        third = squares - first - second
        columns = jnp.where(lane == 0, first, jnp.where(lane == 1, second, jnp.where(lane == 2, third, 0.0)))
        for out, at, rows in blocks_of(outs):
            if at <= to < at + rows:
                out[to - at : to - at + unit, 2 * hidden :] = columns.astype(jnp.bfloat16)


def spread(outs, result, start):
    for out, at, rows in blocks_of(outs):
        out[:, start : start + result.shape[1]] = result[at : at + rows]


def load_gate_up_kernel(order_z, order_y, x_ref, gain_ref, wg_hbm, wu_hbm, *refs):
    outs, scaled, half_sum, wg_ref, wu_ref, sems = refs[:-5], *refs[-5:]
    width, hidden = wg_ref.shape
    half, part = width // 2, width // 4
    groups = []
    for n, (source, target) in enumerate(((wg_hbm, wg_ref), (wu_hbm, wu_ref))):
        for m in range(2):
            rows = [pl.ds(m * half + k * part, part) for k in range(2)]
            groups.append(
                [
                    pltpu.make_async_copy(source.at[row], target.at[row], sems.at[4 * n + 2 * m + k])
                    for k, row in enumerate(rows)
                ]
            )
    for copy in groups[0] + groups[1]:
        copy.start()
    scale_rows((order_z, order_y), x_ref, gain_ref, hidden, outs, scaled)
    for n, w_ref in enumerate((wg_ref, wu_ref)):
        for m in range(2):
            for copy in groups[2 * n + m]:
                copy.wait()
            if n == 0:
                for copy in groups[2 + m]:
                    copy.start()
            k = slice(m * half, (m + 1) * half)
            for start in range(0, hidden, 256):
                at = slice(start, min(start + 256, hidden))
                result = jnp.dot(scaled[:, k], w_ref[k, at], preferred_element_type=jnp.float32)
                if m == 0:
                    half_sum[:, at] = result
                else:
                    spread(outs, (half_sum[:, at] + result).astype(jnp.bfloat16), n * hidden + start)


def gate_up(order_z, order_y, x, gain, w_gate, w_up):
    rows, width = x.shape
    hidden = w_gate.shape[1]
    wide = 2 * hidden + 128
    outs = [jax.ShapeDtypeStruct((rows // 4, wide), jnp.bfloat16)] * 2
    outs += [jax.ShapeDtypeStruct((rows // 8, wide), jnp.bfloat16)] * 4
    w_gate = pltpu.with_memory_space_constraint(w_gate, pltpu.HBM)
    w_up = pltpu.with_memory_space_constraint(w_up, pltpu.HBM)
    return pl.pallas_call(
        load_gate_up_kernel,
        out_shape=outs,
        in_specs=[SMEM] * 2 + [VM] * 2 + [ANY] * 2,
        out_specs=[VM] * 6,
        scratch_shapes=[
            pltpu.VMEM((rows, width), jnp.bfloat16),
            pltpu.VMEM((rows, hidden), jnp.float32),
            pltpu.VMEM(w_gate.shape, w_gate.dtype),
            pltpu.VMEM(w_up.shape, w_up.dtype),
            pltpu.SemaphoreType.DMA((8,)),
        ],
        compiler_params=pltpu.CompilerParams(vmem_limit_bytes=24 * 1024 * 1024),
        cost_estimate=pl.CostEstimate(
            flops=4 * rows * width * hidden, transcendentals=0, bytes_accessed=4 * width * hidden + 4 * rows * hidden
        ),
    )(order_z, order_y, x, gain, w_gate, w_up)


def small_call(kernel, outs, *arrays, after=(), weight=0):
    def body(*refs):
        kernel(*refs[: len(arrays)], *refs[len(arrays) + len(after) :])

    return pl.pallas_call(
        body,
        out_shape=[jax.ShapeDtypeStruct(shape, dtype) for shape, dtype in outs],
        in_specs=[VM] * len(arrays) + [ANY] * len(after),
        out_specs=[VM] * len(outs),
        compiler_params=pltpu.CompilerParams(vmem_limit_bytes=8 * 1024 * 1024),
        cost_estimate=pl.CostEstimate(flops=weight, transcendentals=0, bytes_accessed=0) if weight else None,
    )(*arrays, *after)


def early_sum_kernel(a0, a1, a2, a3, out):
    for start in range(0, out.shape[1], 128):
        at = slice(start, start + 128)
        out[:, at] = f32(a0[:, at]) + f32(a1[:, at]) + f32(a2[:, at]) + f32(a3[:, at])


def line_sum_kernel(early, a0, a1, a2, a3, keep, go):
    unit = keep.shape[0] // 2
    for start in range(0, keep.shape[1], 128):
        at = slice(start, start + 128)
        late = f32(a0[:, at]) + f32(a1[:, at]) + f32(a2[:, at]) + f32(a3[:, at])
        for lo, out in ((0, keep), (unit, go)):
            out[:unit, at] = early[lo : lo + unit, at].astype(out.dtype)
            out[unit:, at] = late[lo : lo + unit].astype(out.dtype)


def pair_sum_kernel(b0, b1, c0, c1, *outs):
    unit = outs[0].shape[0] // 2
    for start in range(0, outs[0].shape[1], 128):
        at = slice(start, start + 128)
        for n, out in enumerate(outs):
            rows = slice(n * unit, (n + 1) * unit)
            out[:unit, at] = (f32(b0[rows, at]) + f32(b1[rows, at])).astype(out.dtype)
            out[unit:, at] = (f32(c0[rows, at]) + f32(c1[rows, at])).astype(out.dtype)


def activate_kernel(keep, *refs):
    others, out = refs[:-1], refs[-1]
    hidden = out.shape[1]

    def summed(start):
        at = slice(start, start + 128)
        value = keep[:, at]
        for other in others:
            value = value + f32(other[:, at])
        return value

    squares = jnp.sum(summed(2 * hidden), axis=1, keepdims=True)
    scale = lax.rsqrt(squares / D + 1e-05) * UP
    for start in range(0, hidden, 128):
        gate = summed(start) * scale
        up = summed(hidden + start) * scale
        out[:, start : start + 128] = (gate / (1.0 + jnp.exp(-gate)) * up).astype(jnp.bfloat16)


def stack_kernel(*refs):
    parts, out = refs[:-1], refs[-1]
    unit = parts[0].shape[0]
    for n, part in enumerate(parts):
        out[n * unit : (n + 1) * unit, :] = part[...]


def put_blocks(order, pieces, target, base, unit):
    per = pieces[0].shape[0] // unit
    for n in range(8):
        start = pl.multiple_of(order[n] * unit, unit)
        at = (n % per) * unit
        target[pl.ds(base + start, unit), :] = pieces[n // per][at : at + unit, :]


def place_kernel(order, *refs):
    put_blocks(order, refs[:-1], refs[-1], 0, refs[-1].shape[0] // 8)


def place(order, pieces, weight):
    rows = sum(piece.shape[0] for piece in pieces)
    return pl.pallas_call(
        place_kernel,
        out_shape=jax.ShapeDtypeStruct((rows, pieces[0].shape[1]), pieces[0].dtype),
        in_specs=[SMEM] + [VM] * len(pieces),
        out_specs=VM,
        compiler_params=pltpu.CompilerParams(vmem_limit_bytes=4 * 1024 * 1024),
        cost_estimate=pl.CostEstimate(flops=weight, transcendentals=0, bytes_accessed=0),
    )(order, *pieces)


def down_kernel(order_b, placed, *refs):
    pieces, w_ref, out_mine, out_other, hidden = refs[:-4], *refs[-4:]
    half = hidden.shape[0] // 2
    unit = half // 16
    per = pieces[0].shape[0] // (2 * unit)
    for n in range(8):
        start = pl.multiple_of(order_b[n] * (2 * unit), 2 * unit)
        at = (n % per) * 2 * unit
        for group in range(2):
            piece = pieces[n // per][at + group * unit : at + (group + 1) * unit, :]
            hidden[pl.ds(group * half + start, unit), :] = piece
            to = group * half + (2 * n + 1) * unit
            hidden[to : to + unit, :] = placed[(2 * n + group) * unit : (2 * n + group + 1) * unit, :]
    for start in range(0, w_ref.shape[1], 256):
        result = jnp.dot(hidden[...], w_ref[:, start : start + 256], preferred_element_type=jnp.float32)
        result = result.astype(jnp.bfloat16)
        out_mine[:, start : start + 256] = result[:half]
        out_other[:, start : start + 256] = result[half:]


def down(order_b, placed, pieces_b, w_down):
    rows = placed.shape[0]
    inner, width = w_down.shape
    return pl.pallas_call(
        down_kernel,
        out_shape=[jax.ShapeDtypeStruct((rows, width), jnp.bfloat16)] * 2,
        in_specs=[SMEM] + [VM] * (len(pieces_b) + 2),
        out_specs=[VM] * 2,
        scratch_shapes=[pltpu.VMEM((2 * rows, inner), jnp.bfloat16)],
        compiler_params=pltpu.CompilerParams(vmem_limit_bytes=10 * 1024 * 1024),
    )(order_b, placed, *pieces_b, w_down)


def qkv_kernel(mine_ref, other_ref, src_ref, dst_ref, w_ref, *refs):
    outs, ordered = refs[:-1], refs[-1]
    half = mine_ref.shape[0]
    pick = jnp.where(dst_ref[...] == src_ref[...], 1.0, 0.0).astype(jnp.bfloat16)
    for start in range(0, mine_ref.shape[1], 512):
        at = slice(start, start + 512)
        rows = jnp.dot(pick[:, :half], mine_ref[:, at], preferred_element_type=jnp.float32)
        rows = rows + jnp.dot(pick[:, half:], other_ref[:, at], preferred_element_type=jnp.float32)
        ordered[:, at] = rows.astype(jnp.bfloat16)
    wide = w_ref.shape[2]
    for part in range(w_ref.shape[0]):
        result = jnp.dot(ordered[...], w_ref[part], preferred_element_type=jnp.float32).astype(jnp.bfloat16)
        spread(outs, result, part * wide)


def slot_qkv(mine, other, key_src, key_dst, w_parts):
    half, width = mine.shape
    rows = 2 * half
    parts, _, wide = w_parts.shape
    return pl.pallas_call(
        qkv_kernel,
        out_shape=[jax.ShapeDtypeStruct((rows // 8, parts * wide), jnp.bfloat16)] * 8,
        in_specs=[VM] * 5,
        out_specs=[VM] * 8,
        scratch_shapes=[pltpu.VMEM((rows, width), jnp.bfloat16)],
        compiler_params=pltpu.CompilerParams(vmem_limit_bytes=12 * 1024 * 1024),
        cost_estimate=pl.CostEstimate(
            flops=2 * rows * width * (parts * wide + rows),
            transcendentals=0,
            bytes_accessed=2 * width * (parts * wide + rows),
        ),
    )(mine, other, key_src, key_dst, w_parts)


def per_device(
    states,
    norm_gain,
    w_gate,
    w_up,
    w_down,
    w_qkv,
    w_class,
    cache_keys,
    cache_values,
    cache_lengths,
    row_slots,
):
    steps = states.shape[0]
    local_rows = states.shape[1]
    width = states.shape[2]
    hidden_here = w_gate.shape[1]
    owner_rows = cache_keys.shape[0]
    history = cache_keys.shape[1]
    local_width = w_qkv.shape[2]
    heads_here = local_width // HEAD_DIM
    total_rows = row_slots.shape[0]
    rows = steps * total_rows
    per = steps * local_rows
    block = rows // 8
    unit = block // 2
    tx = lax.axis_index("tx")
    ty = lax.axis_index("ty")
    my_y, my_zh = tx % 4, tx // 4

    def to(dy, dz):
        return (my_zh ^ dz) * 4 + (my_y + dy) % 4

    def source(dy, dz):
        return (my_zh ^ dz) * 4 + (my_y - dy + 4) % 4

    y_major = [(dy, dz) for dy in range(4) for dz in range(2)]
    z_major = [(dy, dz) for dz in range(2) for dy in range(4)]
    send_a = jnp.stack([to(*m) for m in y_major])
    send_b = jnp.stack([to(*m) for m in z_major])
    from_a = jnp.stack([source(*m) for m in y_major])
    from_b = jnp.stack([source(*m) for m in z_major])

    pos = jnp.arange(rows, dtype=jnp.int32)
    chunk = pos // per
    source_ty = 2 * (chunk % 8) + ((ty % 2) ^ (chunk // 8))
    row_of = source_ty * local_rows + pos % local_rows
    hit = row_of[:, None] == jnp.arange(total_rows, dtype=jnp.int32)[None, :]
    slot_of = jnp.sum(jnp.where(hit, row_slots[None, :], 0), axis=1)
    key_src = (((pos % per) // local_rows) * total_rows + slot_of)[None, :]
    moves = [(0, 0), (2, 1), (1, 1), (3, 1), (2, 0), (0, 1), (1, 0), (3, 0)]
    target = jnp.zeros((rows,), jnp.int32)
    for n, move in enumerate(moves):
        target = jnp.where(pos // block == n, to(*move), target)
    key_dst = ((pos % block) // owner_rows) * total_rows + target * owner_rows + pos % owner_rows
    key_dst = key_dst[:, None]

    own = states.reshape(per, width)
    gain = norm_gain[None, :]
    mine, other = gather_ty(own)
    parts = gate_up(send_b, send_a, mine, gain, w_gate, w_up)
    more = gate_up(send_b, send_a, other, gain, w_gate, w_up)
    half_send = (unit, parts[0].shape[1])
    keep = (half_send, jnp.float32)
    go = (half_send, jnp.bfloat16)
    half_hidden = ((unit, hidden_here), jnp.bfloat16)
    both_b, both_a = [], []
    for group in (parts, more):
        both_b += [group[0], tx_move(group[1], 0, 1)]
        both_a += [group[2]] + [tx_move(group[2 + dy], dy, 0) for dy in (2, 1, 3)]
    (early,) = small_call(early_sum_kernel, [keep], *both_a[:4], weight=5000000000)
    keep_b, *go_b = small_call(pair_sum_kernel, [keep, go, go, go], *both_b, after=(early,))
    came_b = [tx_move(go_b[dy - 1], dy, 0) for dy in (2, 1, 3)]
    keep_a, go_a = small_call(line_sum_kernel, [keep, go], early, *both_a[4:], after=(go_b[0],))
    came_a = tx_move(go_a, 0, 1)
    (hidden_b,) = small_call(activate_kernel, [half_hidden], keep_b, *came_b, after=(go_a,))
    came_b = [tx_move(hidden_b, dy, 0) for dy in (2, 1, 3)]
    (hidden_a,) = small_call(activate_kernel, [half_hidden], keep_a, came_a, after=(hidden_b,))
    came_a = tx_move(hidden_a, 0, 1)
    (pair_a,) = small_call(stack_kernel, [((2 * unit, hidden_here), jnp.bfloat16)], hidden_a, came_a)
    (line_b,) = small_call(
        stack_kernel, [((4 * unit, hidden_here), jnp.bfloat16)], hidden_b, came_b[1], came_b[0], came_b[2], after=(pair_a,)
    )
    pieces_a = [pair_a] + [tx_move(pair_a, dy, 0) for dy in (1, 2, 3)]
    pieces_b = [line_b, tx_move(line_b, 0, 1)]
    w_down = fetch(w_down, 4, pair_a)
    placed = place(from_a, pieces_a, 2500000000)
    mixed_b, mixed_a = down(from_b, placed, pieces_b, w_down)
    chip = (f32(mixed_b) + f32(core_swap(mixed_a))).astype(jnp.bfloat16)
    parts = chip_exchange(chip.reshape(8, per, width))
    stream = (f32(own) + jnp.sum(f32(parts), axis=0)).astype(jnp.bfloat16)
    stream_out = stream.reshape(steps, local_rows, width)

    mine, other = gather_ty(stream)
    w_parts = fetch(jnp.transpose(w_qkv, (1, 0, 2)), 3, mine)
    qkv = slot_qkv(mine, other, key_src, key_dst, w_parts)
    triple = f32(qkv[0])
    for piece, move in zip(qkv[1:], moves[1:]):
        triple = triple + f32(tx_move(piece, *move))
    triple = triple.astype(jnp.bfloat16)
    triple = triple.reshape(steps, owner_rows, 3, heads_here, HEAD_DIM)
    query, new_keys, new_vals = triple[:, :, 0], triple[:, :, 1], triple[:, :, 2]
    keys_h = cache_keys.reshape(owner_rows, history, heads_here, HEAD_DIM)
    vals_h = cache_values.reshape(owner_rows, history, heads_here, HEAD_DIM)
    old = jnp.einsum("tshd,slhd->tshl", query, keys_h, preferred_element_type=jnp.float32)
    new = jnp.einsum("tshd,ushd->tshu", query, new_keys, preferred_element_type=jnp.float32)
    old = old * HEAD_DIM ** (-0.5)
    new = new * HEAD_DIM ** (-0.5)
    where_pos = jnp.arange(history, dtype=jnp.int32)
    old = jnp.where((where_pos[None, :] < cache_lengths[:, None])[None, :, None, :], old, jnp.float32(-1e30))
    causal = jnp.arange(steps)[:, None] >= jnp.arange(steps)[None, :]
    new = jnp.where(causal[:, None, None, :], new, jnp.float32(-1e30))
    top = jnp.maximum(jnp.max(old, axis=3, keepdims=True), jnp.max(new, axis=3, keepdims=True))
    old = jnp.exp(old - top)
    new = jnp.exp(new - top)
    denom = jnp.sum(old, axis=3, keepdims=True) + jnp.sum(new, axis=3, keepdims=True)
    old = (old / denom).astype(jnp.bfloat16)
    new = (new / denom).astype(jnp.bfloat16)
    attended = jnp.einsum("tshl,slhd->tshd", old, vals_h, preferred_element_type=jnp.float32)
    attended = attended + jnp.einsum("tshu,ushd->tshd", new, new_vals, preferred_element_type=jnp.float32)
    attended = attended.reshape(steps * owner_rows, local_width).astype(jnp.bfloat16)
    part = jnp.einsum("rf,fk->kr", attended, w_class, preferred_element_type=jnp.float32)
    classes = part.shape[0]
    packed = jnp.concatenate([part[: classes // 2], part[classes // 2 :]], axis=1)
    packed = jnp.pad(packed, ((0, 1), (0, 0)))
    spread = lax.all_to_all(jnp.broadcast_to(packed[None], (128,) + packed.shape), ("tx", "ty"), 0, 0)
    by_tx = jnp.sum(spread.reshape(8, 16, 8, 128), axis=1)[:, : classes // 2]
    by_tx = by_tx.reshape(8, classes // 2, 2, steps, owner_rows)
    by_slot = by_tx.transpose(2, 1, 3, 0, 4).reshape(classes * steps, total_rows)
    pick = (jnp.arange(total_rows)[:, None] == row_slots[None, :]).astype(jnp.float32)
    logits = jnp.dot(by_slot, pick, precision=lax.Precision.HIGHEST, preferred_element_type=jnp.float32)
    category_logits = logits.reshape(classes, steps, total_rows).transpose(1, 2, 0)
    return (stream_out, category_logits)


def solution(mesh):
    return jax.shard_map(
        per_device,
        mesh=mesh,
        in_specs=(
            P(None, "ty", "tx"),
            P("tx"),
            P("tx", "ty"),
            P("tx", "ty"),
            P("ty", "tx"),
            P("tx", None, "ty"),
            P("ty", None),
            P("tx", None, "ty"),
            P("tx", None, "ty"),
            P("tx"),
            P(),
        ),
        out_specs=(P(None, "ty", "tx"), P()),
        check_vma=False,
    )
```
